256 devices in a mesh: space: 4 (over x_hi, core), orient: 64 (over x_lo, y, z).
Axes of the slice: x: 4 (x_hi: 2, x_lo: 2; x = x_hi * 2 + x_lo), y: 4, z: 8, core: 2. Of those that a mesh axis runs over, the one named last changes fastest.
Arguments:
- q_init: bfloat16 [256, 64, 128, 128], P('orient', 'space'), may hold values from 0.5 to 1.5
- partner: bfloat16 [256, 64, 128, 128], P('orient', 'space'), may hold values from 0.5 to 1.5
- field: bfloat16 [6, 64, 128, 128], P(None, 'space'), may hold values from -3 to 3
- orientations: float32 [3, 256], replicated, may hold values from -1 to 1, as said below
- orient_weight: float32 [256], replicated, may hold values from 0.03 to 0.12
- rotation: bfloat16 [256, 256], replicated, may hold values from -1 to 1
Outputs:
- q_final: bfloat16 [256, 64, 128, 128], P('orient', 'space')
- new_field: float32 [6, 64, 128, 128], P(None, 'space', 'orient')
The draws below stay inside these ranges and needn't reach their ends.
Inputs may be any that keep to these rules, and one draw needn't show every extreme that they name: `orientations`: each column is a unit vector.
All inputs are finite; a program needn't handle non-finite values.
Results may differ from the reference program's by a relative error of at most 0.0057.
Values may be sent and summed in bfloat16 or wider, within the bound.
A program may use at most 128 MiB of HBM per device.

```python
import math
import jax
import jax.numpy as jnp
from jax import lax

NO = 256
NX = 128
NY = 128
STEPS = 2
NZ = 64


def draw_orientations(key, part):
    raw = jax.random.normal(key, (3, NO), jnp.float32)
    return raw / jnp.sqrt(jnp.sum(raw * raw, axis=0, keepdims=True))


def draw_rotation(key, part):
    spread = jax.random.normal(key, (NO, NO), jnp.float32)
    spread = jnp.clip(spread, -4.0, 4.0)
    return (0.6 * jnp.eye(NO, dtype=jnp.float32) + 0.4 * spread / jnp.sqrt(NO * 1.0)).astype(jnp.bfloat16)


def block_levels(stream_key, dims, pieces, low, high):
    def one(position, blocks):
        draws = jax.random.uniform(jax.random.fold_in(jax.random.fold_in(stream_key, 6), position), (blocks,), jnp.float32, low / len(pieces), high / len(pieces))
        return jnp.repeat(jnp.exp(draws), dims[position] // blocks).reshape((-1,) + (1,) * (len(dims) - position - 1))

    gain = one(*pieces[0])
    for cut in pieces[1:]:
        gain = gain * one(*cut)
    return gain


def centred(key, shape, width, bound, shards=(), kind=jnp.bfloat16):
    loudness = block_levels(key, shape, shards, -0.22, 0.18) if shards else 1.0
    values = jax.random.normal(key, shape, jnp.float32) * width * loudness
    return jnp.minimum(jnp.maximum(values, -bound), bound).astype(kind)


def setup_inputs(seed: int = 0) -> dict:
    streams_of = jax.random.split(jax.random.key(seed), 7)
    return {
        "q_init": jnp.clip(0.5 + 1.0 * jax.random.uniform(streams_of[0], (NO, NZ, NY, NX), jnp.float32) ** block_levels(streams_of[0], (NO, NZ, NY, NX), ((0, 64), (1, 4)), -0.2, 0.2), 0.5, 1.5).astype(jnp.bfloat16),
        "partner": jnp.clip(0.5 + 1.0 * jax.random.uniform(streams_of[1], (NO, NZ, NY, NX), jnp.float32) ** block_levels(streams_of[1], (NO, NZ, NY, NX), ((0, 64), (1, 4)), -0.2, 0.2), 0.5, 1.5).astype(jnp.bfloat16),
        "field": centred(streams_of[2], (6, NZ, NY, NX), 0.5, 3.0, ((1, 4),)),
        "orientations": draw_orientations(jax.random.fold_in(streams_of[6], 71), 0),
        "orient_weight": jnp.clip(jnp.exp(jax.random.uniform(streams_of[4], (NO,), jnp.float32, math.log(0.03), math.log(0.12))), 0.03, 0.12),
        "rotation": draw_rotation(jax.random.fold_in(streams_of[6], 71), 0),
    }


step_length = 0.3
relax_rate = 0.5
coupling = 8.0


def angle_tables(orientations):
    along_x = orientations[0]
    along_y = orientations[1]
    along_z = orientations[2]
    field_terms = jnp.stack([along_x * along_x, along_y * along_y, along_z * along_z, 2.0 * along_x * along_y, 2.0 * along_x * along_z, 2.0 * along_y * along_z])
    tensor_terms = jnp.stack([along_x * along_x - 1.0 / 3.0, along_y * along_y - 1.0 / 3.0, along_z * along_z - 1.0 / 3.0, along_x * along_y, along_x * along_z, along_y * along_z])
    return field_terms, tensor_terms


def upwind(center, below, above, speeds):
    speed_x, speed_y, speed_z = speeds
    back_x = center - jnp.roll(center, 1, axis=-1)
    fore_x = jnp.roll(center, -1, axis=-1) - center
    back_y = center - jnp.roll(center, 1, axis=-2)
    fore_y = jnp.roll(center, -1, axis=-2) - center
    back_z = center - below
    fore_z = above - center
    total = jnp.maximum(speed_x, 0.0) * back_x + jnp.minimum(speed_x, 0.0) * fore_x
    total = total + jnp.maximum(speed_y, 0.0) * back_y + jnp.minimum(speed_y, 0.0) * fore_y
    total = total + jnp.maximum(speed_z, 0.0) * back_z + jnp.minimum(speed_z, 0.0) * fore_z
    return center - step_length * total


def reference(q_init, partner, field, orientations, orient_weight, rotation):
    field_terms, tensor_terms = angle_tables(orientations)
    wide_field = field.astype(jnp.float32)

    def advect_one(inputs):
        block, speeds, terms = inputs
        center = block.astype(jnp.float32)
        below = jnp.roll(center, 1, axis=0)
        above = jnp.roll(center, -1, axis=0)
        moved = upwind(center, below, above, (speeds[0], speeds[1], speeds[2]))
        potential = jnp.tensordot(terms, wide_field, axes=1, precision=lax.Precision.HIGHEST)
        return (moved * jnp.exp(-step_length * potential)).astype(jnp.bfloat16)

    def rotate_slice(layer):
        flat = layer.reshape(layer.shape[0], -1)
        return jnp.dot(rotation, flat, preferred_element_type=jnp.float32).astype(jnp.bfloat16).reshape(layer.shape)

    state = q_init
    for contour in range(STEPS):
        advected = lax.map(advect_one, (state, orientations.T, field_terms.T))
        turned = lax.map(rotate_slice, jnp.moveaxis(advected, 1, 0))
        state = jnp.moveaxis(turned, 0, 1)

    all_terms = tensor_terms * orient_weight[None, :]

    def tensor_slice(inputs):
        layer, other = inputs
        product = layer.astype(jnp.float32) * other.astype(jnp.float32)
        sums = jnp.dot(all_terms, product.reshape(product.shape[0], -1), precision=lax.Precision.HIGHEST)
        return sums.reshape((6,) + product.shape[1:])

    tensor = lax.map(tensor_slice, (jnp.moveaxis(state, 1, 0), jnp.moveaxis(partner, 1, 0)))
    tensor = jnp.moveaxis(tensor, 0, 1)
    new_field = (1.0 - relax_rate) * wide_field + relax_rate * coupling * tensor
    return state, new_field
```

```python
import functools

import jax
import jax.numpy as jnp
from jax import lax
from jax.experimental import pallas as pl
from jax.experimental.pallas import tpu as pltpu
from jax.sharding import PartitionSpec as P

step_length = 0.3
relax_rate = 0.5
coupling = 8.0

ZT = 2
YT = 16


def angle_tables(orientations):
    ux, uy, uz = orientations[0], orientations[1], orientations[2]
    field_terms = jnp.stack(
        [ux * ux, uy * uy, uz * uz, 2.0 * ux * uy, 2.0 * ux * uz, 2.0 * uy * uz]
    )
    third = 1.0 / 3.0
    tensor_terms = jnp.stack(
        [ux * ux - third, uy * uy - third, uz * uz - third, ux * uy, ux * uz, uy * uz]
    )
    return field_terms, tensor_terms


def split3(values):
    high = lax.reduce_precision(values, 8, 7)
    rest = values - high
    mid = lax.reduce_precision(rest, 8, 7)
    low = rest - mid
    return [piece.astype(jnp.bfloat16) for piece in (high, mid, low)]


def advect_kernel(zt, yt, coef_ref, q_ref, lo_ref, hi_ref, hlo_ref, hhi_ref, w_ref, out_ref):
    step = pl.program_id(0)
    last = pl.num_programs(0) - 1
    count = q_ref.shape[0]
    ny = q_ref.shape[2]
    nx = q_ref.shape[3]
    for zz in range(zt):
        planes = [w_ref[c, zz].astype(jnp.float32) for c in range(6)]
        for o in range(count):
            f = q_ref[o, zz].astype(jnp.float32)
            if zz > 0:
                below = q_ref[o, zz - 1].astype(jnp.float32)
            else:
                below = jnp.where(step == 0, hlo_ref[o, 0], lo_ref[o, 0]).astype(jnp.float32)
            if zz < zt - 1:
                above = q_ref[o, zz + 1].astype(jnp.float32)
            else:
                above = jnp.where(step == last, hhi_ref[o, 0], hi_ref[o, 0]).astype(jnp.float32)
            positive = [coef_ref[o, 10 + a] > 0.0 for a in range(3)]
            up_x = pltpu.roll(f, jnp.where(positive[0], 1, nx - 1), 1)
            up_y = jnp.where(positive[1], pltpu.roll(f, 1, 0), pltpu.roll(f, ny - 1, 0))
            up_z = jnp.where(positive[2], below, above)
            moved = f * coef_ref[o, 9]
            moved = moved + coef_ref[o, 6] * up_x
            moved = moved + coef_ref[o, 7] * up_y
            moved = moved + coef_ref[o, 8] * up_z
            power = coef_ref[o, 0] * planes[0]
            for c in range(1, 6):
                power = power + coef_ref[o, c] * planes[c]
            res = (moved * jnp.exp(power)).astype(jnp.bfloat16)
            for yb in range(ny // yt):
                out_ref[yb, 0, o, zz] = res[yb * yt : (yb + 1) * yt]


def rotate_kernel(yt, rot_ref, in_ref, out_ref, wide):
    no = in_ref.shape[0]
    nx = in_ref.shape[3]
    wide[...] = in_ref[:, 0].astype(jnp.float32).reshape(no * yt, nx)

    def body(y, carry):
        tile = wide[pl.ds(y, no, stride=yt), :].astype(jnp.bfloat16)
        turned = jnp.dot(rot_ref[...], tile, preferred_element_type=jnp.float32)
        out_ref[0, y] = turned.astype(jnp.bfloat16)
        return carry

    lax.fori_loop(0, yt, body, 0)


def second_kernel(
    zt,
    yt,
    rot_ref,
    coef_ref,
    ft_ref,
    tt_ref,
    q_ref,
    zlo_ref,
    zhi_ref,
    ylo_ref,
    yhi_ref,
    w_ref,
    part_ref,
    out_ref,
    field_ref,
    ext,
    wide,
    pwide,
):
    z = pl.program_id(0)
    no = q_ref.shape[2]
    nx = q_ref.shape[3]

    @pl.when(z == 0)
    def fill():
        for zz in range(zt):
            ext[zz + 1, 0] = ylo_ref[zz]
            ext[zz + 1, yt + 1] = yhi_ref[zz]
            for y in range(yt):
                ext[zz + 1, y + 1] = q_ref[zz, y]
        for y in range(yt):
            ext[0, y + 1] = zlo_ref[y]
            ext[zt + 1, y + 1] = zhi_ref[y]

    pwide[...] = part_ref[:, 0].astype(jnp.float32).reshape(no * yt, nx)

    def body(y, carry):
        f = ext[z + 1, y + 1].astype(jnp.float32)
        up_x = jnp.where(coef_ref[4] > 0, pltpu.roll(f, 1, 1), pltpu.roll(f, nx - 1, 1))
        up_y = jnp.where(
            coef_ref[5] > 0,
            ext[z + 1, y].astype(jnp.float32),
            ext[z + 1, y + 2].astype(jnp.float32),
        )
        up_z = jnp.where(
            coef_ref[6] > 0,
            ext[z, y + 1].astype(jnp.float32),
            ext[z + 2, y + 1].astype(jnp.float32),
        )
        moved = f * coef_ref[0] + coef_ref[1] * up_x + coef_ref[2] * up_y + coef_ref[3] * up_z
        w = w_ref[0, y]
        power = jnp.dot(ft_ref[...], w, preferred_element_type=jnp.float32)
        adv = (moved * jnp.exp(power)).astype(jnp.bfloat16)
        turned = jnp.dot(rot_ref[...], adv, preferred_element_type=jnp.float32)
        q2 = turned.astype(jnp.bfloat16).astype(jnp.float32)
        wide[pl.ds(y, no, stride=yt), :] = q2
        prod = q2 * pwide[pl.ds(y, no, stride=yt), :]
        high = prod.astype(jnp.bfloat16)
        low = (prod - high.astype(jnp.float32)).astype(jnp.bfloat16)
        sums = jnp.dot(tt_ref[...], high, preferred_element_type=jnp.float32)
        sums = sums + jnp.dot(tt_ref[...], low, preferred_element_type=jnp.float32)
        total = sums[0:8] + sums[8:16] + sums[16:24]
        old = w[0:8].astype(jnp.float32)
        field_ref[0, y] = (1.0 - relax_rate) * old + relax_rate * coupling * total
        return carry

    lax.fori_loop(0, yt, body, 0)
    out_ref[:, 0] = wide[...].astype(jnp.bfloat16).reshape(no, yt, nx)


def per_device(q_init, partner, field, orientations, orient_weight, rotation):
    count, nz, ny, nx = q_init.shape
    no = orientations.shape[1]
    zt, yt = ZT, YT
    nzb, nyb = nz // zt, ny // yt
    groups = nzb * nyb
    spaces = lax.axis_size("space")
    bf16 = jnp.bfloat16

    me = lax.axis_index("orient")
    my_yb = me // nzb
    my_zb = me % nzb

    field_terms, tensor_terms = angle_tables(orientations)
    magnitude = step_length * jnp.abs(orientations)
    rest = 1.0 - (magnitude[0] + magnitude[1] + magnitude[2])
    sign = jnp.where(orientations > 0.0, 1.0, 0.0)
    scaled = -step_length * field_terms

    packed = jnp.concatenate([scaled, magnitude, rest[None], sign, jnp.zeros((3, no))], axis=0)
    local = lax.dynamic_slice_in_dim(packed, me * count, count, 1).T

    forward = [(i, (i + 1) % spaces) for i in range(spaces)]
    backward = [(b, a) for a, b in forward]
    halo_lo = lax.ppermute(q_init[:, -1:], "space", forward)
    halo_hi = lax.ppermute(q_init[:, :1], "space", backward)

    plane = (count, 1, ny, nx)
    advected = pl.pallas_call(
        functools.partial(advect_kernel, zt, yt),
        grid=(nzb,),
        in_specs=[
            pl.BlockSpec(memory_space=pltpu.SMEM),
            pl.BlockSpec((count, zt, ny, nx), lambda i: (0, i, 0, 0)),
            pl.BlockSpec(plane, lambda i: (0, jnp.maximum(i * zt - 1, 0), 0, 0)),
            pl.BlockSpec(plane, lambda i: (0, jnp.minimum(i * zt + zt, nz - 1), 0, 0)),
            pl.BlockSpec(plane, lambda i: (0, 0, 0, 0)),
            pl.BlockSpec(plane, lambda i: (0, 0, 0, 0)),
            pl.BlockSpec((6, zt, ny, nx), lambda i: (0, i, 0, 0)),
        ],
        out_specs=pl.BlockSpec((nyb, 1, count, zt, yt, nx), lambda i: (0, i, 0, 0, 0, 0)),
        out_shape=jax.ShapeDtypeStruct((nyb, nzb, count, zt, yt, nx), bf16),
        compiler_params=pltpu.CompilerParams(vmem_limit_bytes=32 << 20),
        name="advect",
    )(local, q_init, q_init, q_init, halo_lo, halo_hi, field)

    def exchange(blocks):
        return lax.all_to_all(blocks, "orient", split_axis=0, concat_axis=0, tiled=True)

    part = partner.reshape(count, nzb, zt, nyb, yt, nx).transpose(3, 1, 0, 2, 4, 5)
    part = exchange(part.reshape(groups, count, zt, yt, nx)).reshape(no, zt, yt, nx)
    got = exchange(advected.reshape(groups, count, zt, yt, nx)).reshape(no, zt, yt, nx)

    state = pl.pallas_call(
        functools.partial(rotate_kernel, yt),
        grid=(zt,),
        in_specs=[
            pl.BlockSpec((no, no), lambda i: (0, 0)),
            pl.BlockSpec((no, 1, yt, nx), lambda i: (0, i, 0, 0)),
        ],
        out_specs=pl.BlockSpec((1, yt, no, nx), lambda i: (i, 0, 0, 0)),
        out_shape=jax.ShapeDtypeStruct((zt, yt, no, nx), bf16),
        scratch_shapes=[pltpu.VMEM((no * yt, nx), jnp.float32)],
        compiler_params=pltpu.CompilerParams(vmem_limit_bytes=32 << 20),
        name="rotate",
    )(rotation, got)

    z_next = []
    y_next = []
    for s in range(spaces):
        for yb in range(nyb):
            for zb in range(nzb):
                src = s * groups + yb * nzb + zb
                if zb < nzb - 1:
                    dst = src + 1
                else:
                    dst = ((s + 1) % spaces) * groups + yb * nzb
                z_next.append((src, dst))
                y_next.append((src, s * groups + ((yb + 1) % nyb) * nzb + zb))
    z_prev = [(b, a) for a, b in z_next]
    y_prev = [(b, a) for a, b in y_next]
    both = ("space", "orient")
    zlo = lax.ppermute(state[zt - 1], both, z_next)
    zhi = lax.ppermute(state[0], both, z_prev)
    ylo = lax.ppermute(state[:, yt - 1], both, y_next)
    yhi = lax.ppermute(state[:, 0], both, y_prev)

    own = lax.dynamic_slice(field, (0, my_zb * zt, my_yb * yt, 0), (6, zt, yt, nx))
    own = jnp.pad(own.transpose(1, 2, 0, 3), ((0, 0), (0, 0), (0, 2), (0, 0)))
    own3 = jnp.concatenate([own, own, own], axis=2)
    ft = jnp.pad(scaled.T, ((0, 0), (0, 2)))
    ft3 = jnp.concatenate(split3(ft), axis=1)
    tt = jnp.pad(tensor_terms * orient_weight[None, :], ((0, 2), (0, 0)))
    tt3 = jnp.concatenate(split3(tt), axis=0)
    wide_coef = jnp.concatenate([rest[None], magnitude, sign], axis=0)
    wide_coef = jnp.broadcast_to(wide_coef[:, :, None], (7, no, nx))

    full = lambda *shape: pl.BlockSpec(shape, lambda i: (0,) * len(shape))
    back, new_block = pl.pallas_call(
        functools.partial(second_kernel, zt, yt),
        grid=(zt,),
        in_specs=[
            full(no, no),
            full(7, no, nx),
            full(no, 24),
            full(24, no),
            full(zt, yt, no, nx),
            full(yt, no, nx),
            full(yt, no, nx),
            full(zt, no, nx),
            full(zt, no, nx),
            pl.BlockSpec((1, yt, 24, nx), lambda i: (i, 0, 0, 0)),
            pl.BlockSpec((no, 1, yt, nx), lambda i: (0, i, 0, 0)),
        ],
        out_specs=[
            pl.BlockSpec((no, 1, yt, nx), lambda i: (0, i, 0, 0)),
            pl.BlockSpec((1, yt, 8, nx), lambda i: (i, 0, 0, 0)),
        ],
        out_shape=[
            jax.ShapeDtypeStruct((no, zt, yt, nx), bf16),
            jax.ShapeDtypeStruct((zt, yt, 8, nx), jnp.float32),
        ],
        scratch_shapes=[
            pltpu.VMEM((zt + 2, yt + 2, no, nx), bf16),
            pltpu.VMEM((no * yt, nx), jnp.float32),
            pltpu.VMEM((no * yt, nx), jnp.float32),
        ],
        compiler_params=pltpu.CompilerParams(vmem_limit_bytes=48 << 20),
        name="second",
    )(rotation, wide_coef, ft3, tt3, state, zlo, zhi, ylo, yhi, own3, part)

    final = exchange(back.reshape(groups, count, zt, yt, nx))
    final = final.reshape(nyb, nzb, count, zt, yt, nx).transpose(2, 1, 3, 0, 4, 5)
    final = final.reshape(count, nz, ny, nx)

    pairs = ny // groups
    each = yt // pairs
    rows = new_block[:, :, :6].reshape(zt, each, pairs, 6, nx).transpose(1, 3, 0, 2, 4)
    clusters = [[g * nzb + j for j in range(nzb)] for g in range(nyb)]
    rows = lax.all_to_all(
        rows, "orient", split_axis=0, concat_axis=0, axis_index_groups=clusters, tiled=True
    )
    rows = rows.transpose(1, 0, 2, 3, 4).reshape(6, nz, pairs, nx)
    return final, rows


def solution(mesh):
    in_specs = (
        P("orient", "space", None, None),
        P("orient", "space", None, None),
        P(None, "space", None, None),
        P(),
        P(),
        P(),
    )
    out_specs = (P("orient", "space", None, None), P(None, "space", "orient", None))
    return jax.shard_map(
        per_device, mesh=mesh, in_specs=in_specs, out_specs=out_specs, check_vma=False
    )
```

```python
import functools

import jax
import jax.numpy as jnp
from jax import lax
from jax.experimental import pallas as pl
from jax.experimental.pallas import tpu as pltpu
from jax.sharding import PartitionSpec as P

step_length = 0.3
relax_rate = 0.5
coupling = 8.0

F32 = jnp.float32
BF16 = jnp.bfloat16
MESH = pl.DeviceIdType.MESH
ZT = 2
YT = 16
CHUNKS = 4


def whole_kernel(
    dims,
    q_hbm,
    part_hbm,
    w_hbm,
    ub_ref,
    rot_ref,
    dirs,
    weight,
    out_hbm,
    nf_hbm,
    qext,
    wv,
    send1,
    recv1,
    ext,
    wide,
    precv,
    send2,
    nfb,
    cf,
    ft3,
    wown,
    acc,
    sem_in,
    sem_hq,
    sem_hqs,
    sem_r1,
    sem_s1,
    sem_rp,
    sem_sp,
    sem_hz,
    sem_hzs,
    sem_hy,
    sem_hys,
    sem_r2,
    sem_s2,
    sem_rn,
    sem_sn,
):
    spaces, groups, nzb, nyb, count, nz, ny, nx = dims
    no = groups * count
    zt, yt = ZT, YT
    per = yt // CHUNKS
    me = lax.axis_index("orient")
    sp = lax.axis_index("space")
    my_zb = me // nyb
    my_yb = me % nyb
    sp_next = lax.rem(sp + 1, spaces)
    sp_prev = lax.rem(sp + spaces - 1, spaces)
    up = my_zb + 1
    z_next = (lax.rem(sp + up // nzb, spaces), lax.rem(up, nzb) * nyb + my_yb)
    down = my_zb + nzb - 1
    z_prev = (
        lax.rem(sp + spaces - 1 + down // nzb, spaces),
        lax.rem(down, nzb) * nyb + my_yb,
    )
    y_next = (sp, my_zb * nyb + lax.rem(my_yb + 1, nyb))
    y_prev = (sp, my_zb * nyb + lax.rem(my_yb + nyb - 1, nyb))

    load_q = pltpu.make_async_copy(q_hbm, qext.at[:, pl.ds(1, nz)], sem_in.at[0])
    load_w = pltpu.make_async_copy(w_hbm, wv, sem_in.at[1])
    load_q.start()
    load_w.start()

    barrier = pltpu.get_barrier_semaphore()

    def greet(i, carry):
        peer = lax.rem(me + i, groups)
        pl.semaphore_signal(barrier, 1, device_id=(sp, peer), device_id_type=MESH)
        return carry

    for target in (z_next, z_prev, (sp_next, me), (sp_prev, me)):
        pl.semaphore_signal(barrier, 1, device_id=target, device_id_type=MESH)
    lax.fori_loop(1, groups, greet, 0)
    pl.semaphore_wait(barrier, groups + 3)

    def remote(src, dst, ssem, rsem, target):
        return pltpu.make_async_remote_copy(
            src_ref=src,
            dst_ref=dst,
            send_sem=ssem,
            recv_sem=rsem,
            device_id=target,
            device_id_type=MESH,
        )

    remote(
        q_hbm.at[:, pl.ds(nz - 1, 1)], qext.at[:, pl.ds(0, 1)], sem_hqs, sem_hq.at[0], (sp_next, me)
    ).start()
    remote(
        q_hbm.at[:, pl.ds(0, 1)], qext.at[:, pl.ds(nz + 1, 1)], sem_hqs, sem_hq.at[1], (sp_prev, me)
    ).start()

    load_q.wait()
    load_w.wait()

    for p in range(zt):

        def advect_plane(i, carry, p=p):
            zb = lax.rem(my_zb + 1 + i, nzb)
            z = zb * zt + p
            if p == 0:

                @pl.when(zb == 0)
                def low_halo():
                    pltpu.make_async_copy(
                        qext.at[:, pl.ds(0, 1)], qext.at[:, pl.ds(0, 1)], sem_hq.at[0]
                    ).wait()

            if p == zt - 1:

                @pl.when(zb == nzb - 1)
                def high_halo():
                    pltpu.make_async_copy(
                        qext.at[:, pl.ds(nz + 1, 1)], qext.at[:, pl.ds(nz + 1, 1)], sem_hq.at[1]
                    ).wait()

            planes = [wv[c, z].astype(F32) for c in range(6)]
            for o in range(count):
                ux = dirs[0, me * count + o]
                uy = dirs[1, me * count + o]
                uz = dirs[2, me * count + o]
                ax = step_length * jnp.maximum(ux, -ux)
                ay = step_length * jnp.maximum(uy, -uy)
                az = step_length * jnp.maximum(uz, -uz)
                terms = (ux * ux, uy * uy, uz * uz, 2.0 * ux * uy, 2.0 * ux * uz, 2.0 * uy * uz)
                f = qext[o, z + 1].astype(F32)
                below = qext[o, z].astype(F32)
                above = qext[o, z + 2].astype(F32)
                up_x = jnp.where(ux > 0.0, pltpu.roll(f, 1, 1), pltpu.roll(f, nx - 1, 1))
                up_y = jnp.where(uy > 0.0, pltpu.roll(f, 1, 0), pltpu.roll(f, ny - 1, 0))
                up_z = jnp.where(uz > 0.0, below, above)
                moved = f * (1.0 - (ax + ay + az)) + ax * up_x + ay * up_y + az * up_z
                power = (-step_length * terms[0]) * planes[0]
                for c in range(1, 6):
                    power = power + (-step_length * terms[c]) * planes[c]
                res = (moved * jnp.exp(power)).astype(BF16)
                for yb in range(nyb):
                    send1[p, zb * nyb + yb, o] = res[yb * yt : (yb + 1) * yt]

            def ship(j, inner):
                yb = lax.rem(my_yb + 1 + j, nyb)
                d = zb * nyb + yb

                @pl.when(d == me)
                def keep():
                    pltpu.make_async_copy(send1.at[p, d], recv1.at[p, me], sem_r1.at[p]).start()

                @pl.when(d != me)
                def send():
                    remote(
                        send1.at[p, d], recv1.at[p, me], sem_s1, sem_r1.at[p], (sp, d)
                    ).start()

                return inner

            lax.fori_loop(0, nyb, ship, 0)
            return carry

        lax.fori_loop(0, nzb, advect_plane, 0)

    def part_block(d):
        return part_hbm.at[:, pl.ds((d // nyb) * zt, zt), pl.ds(lax.rem(d, nyb) * yt, yt)]

    def ship_part(i, carry):
        d = lax.rem(me + i, groups)
        remote(part_block(d), precv.at[me], sem_sp, sem_rp, (sp, d)).start()
        return carry

    lax.fori_loop(1, groups, ship_part, 0)
    pltpu.make_async_copy(part_block(me), precv.at[me], sem_rp).start()

    ux = ub_ref[0]
    uy = ub_ref[1]
    uz = ub_ref[2]
    ax = step_length * jnp.abs(ux)
    ay = step_length * jnp.abs(uy)
    az = step_length * jnp.abs(uz)
    cf[0] = 1.0 - (ax + ay + az)
    cf[1] = ax
    cf[2] = ay
    cf[3] = az
    lane = lax.broadcasted_iota(jnp.int32, (no, nx), 1)
    terms = (ux * ux, uy * uy, uz * uz, 2.0 * ux * uy, 2.0 * ux * uz, 2.0 * uy * uz)
    packed = jnp.zeros((no, nx), F32)
    for c in range(6):
        value = -step_length * terms[c]
        high = value.astype(BF16).astype(F32)
        rest = value - high
        mid = rest.astype(BF16).astype(F32)
        low = rest - mid
        packed = jnp.where(lane == c, high, packed)
        packed = jnp.where(lane == 8 + c, mid, packed)
        packed = jnp.where(lane == 16 + c, low, packed)
    ft3[...] = packed.astype(BF16)

    wown[...] = jnp.zeros_like(wown)
    for p in range(zt):
        for c in range(6):
            block = wv[c, my_zb * zt + p, pl.ds(pl.multiple_of(my_yb * yt, yt), yt)]
            wown[pl.ds(p * yt * 8 + c, yt, stride=8), :] = block.astype(F32)

    for p in range(zt):
        pltpu.make_async_copy(recv1.at[p], recv1.at[p], sem_r1.at[p]).wait()

        def widen(s, carry, p=p):
            rows = count * yt
            wide[pl.ds(pl.multiple_of(s * rows, rows), rows), :] = (
                recv1[p, s].astype(F32).reshape(rows, nx)
            )
            return carry

        lax.fori_loop(0, groups, widen, 0, unroll=4)
        for chunk in range(CHUNKS):

            def turn(k, carry, p=p, chunk=chunk):
                y = chunk * per + k
                tile = wide[pl.ds(y, no, stride=yt), :].astype(BF16)
                turned = jnp.dot(rot_ref[...], tile, preferred_element_type=F32)
                ext[p + 1, y + 1] = turned.astype(BF16)
                return carry

            lax.fori_loop(0, per, turn, 0, unroll=2)
            rows = pl.ds(1 + chunk * per, per)
            if p == 0:
                remote(
                    ext.at[1, rows], ext.at[zt + 1, rows], sem_hzs, sem_hz.at[1, chunk], z_prev
                ).start()
            if p == zt - 1:
                remote(
                    ext.at[zt, rows], ext.at[0, rows], sem_hzs, sem_hz.at[0, chunk], z_next
                ).start()
            if chunk == 0:
                remote(
                    ext.at[p + 1, pl.ds(1, 1)],
                    ext.at[p + 1, pl.ds(yt + 1, 1)],
                    sem_hys,
                    sem_hy.at[1, p],
                    y_prev,
                ).start()
            if chunk == CHUNKS - 1:
                remote(
                    ext.at[p + 1, pl.ds(yt, 1)],
                    ext.at[p + 1, pl.ds(0, 1)],
                    sem_hys,
                    sem_hy.at[0, p],
                    y_next,
                ).start()

    for p in reversed(range(zt)):
        for side, row in ((0, 0), (1, yt + 1)):
            face = ext.at[p + 1, pl.ds(row, 1)]
            pltpu.make_async_copy(face, face, sem_hy.at[side, p]).wait()
        for chunk in range(CHUNKS):
            rows = pl.ds(1 + chunk * per, per)
            if p == zt - 1:
                face = ext.at[zt + 1, rows]
                pltpu.make_async_copy(face, face, sem_hz.at[1, chunk]).wait()
            if p == 0:
                face = ext.at[0, rows]
                pltpu.make_async_copy(face, face, sem_hz.at[0, chunk]).wait()

            def step(k, carry, p=p, chunk=chunk):
                y = chunk * per + k
                f = ext[p + 1, y + 1].astype(F32)
                up_x = jnp.where(ub_ref[0] > 0.0, pltpu.roll(f, 1, 1), pltpu.roll(f, nx - 1, 1))
                up_y = jnp.where(
                    ub_ref[1] > 0.0, ext[p + 1, y].astype(F32), ext[p + 1, y + 2].astype(F32)
                )
                up_z = jnp.where(
                    ub_ref[2] > 0.0, ext[p, y + 1].astype(F32), ext[p + 2, y + 1].astype(F32)
                )
                moved = f * cf[0] + cf[1] * up_x + cf[2] * up_y + cf[3] * up_z
                w8 = wown[pl.ds(pl.multiple_of((p * yt + y) * 8, 8), 8), :]
                w24 = jnp.concatenate([w8, w8, w8], axis=0).astype(BF16)
                power = jnp.dot(ft3[:, :24], w24, preferred_element_type=F32)
                adv = (moved * jnp.exp(power)).astype(BF16)
                turned = jnp.dot(rot_ref[...], adv, preferred_element_type=F32)
                wide[pl.ds(y, no, stride=yt), :] = turned
                return carry

            lax.fori_loop(0, per, step, 0)

        def ship_home(i, carry, p=p):
            d = lax.rem(me + 1 + i, groups)
            rows = count * yt
            block = wide[pl.ds(pl.multiple_of(d * rows, rows), rows), :]
            send2[p, d] = block.astype(BF16).reshape(count, yt, nx)
            home = out_hbm.at[:, my_zb * zt + p, pl.ds(pl.multiple_of(my_yb * yt, yt), yt)]

            @pl.when(d == me)
            def keep():
                pltpu.make_async_copy(send2.at[p, d], home, sem_r2).start()

            @pl.when(d != me)
            def send():
                remote(send2.at[p, d], home, sem_s2, sem_r2, (sp, d)).start()

            return carry

        lax.fori_loop(0, groups, ship_home, 0)

    pltpu.make_async_copy(precv, precv, sem_rp).wait()
    for p in range(zt):

        def add_terms(d, sums, p=p):
            sums = list(sums)
            for o in range(count):
                gx = dirs[0, d * count + o]
                gy = dirs[1, d * count + o]
                gz = dirs[2, d * count + o]
                gw = weight[d * count + o]
                third = 1.0 / 3.0
                factors = (
                    (gx * gx - third) * gw,
                    (gy * gy - third) * gw,
                    (gz * gz - third) * gw,
                    gx * gy * gw,
                    gx * gz * gw,
                    gy * gz * gw,
                )
                prod = send2[p, d, o].astype(F32) * precv[d, o, p].astype(F32)
                for c in range(6):
                    sums[c] = sums[c] + factors[c] * prod
            return tuple(sums)

        sums = lax.fori_loop(
            0, groups, add_terms, tuple(jnp.zeros((yt, nx), F32) for c in range(6))
        )
        for c in range(6):
            old = wv[c, my_zb * zt + p, pl.ds(pl.multiple_of(my_yb * yt, yt), yt)].astype(F32)
            acc[...] = (1.0 - relax_rate) * old + relax_rate * coupling * sums[c]
            for j in range(nyb):
                nfb[j, c, p] = acc[pl.ds(2 * j, 2), :]

    nf_home = nf_hbm.at[:, pl.ds(my_zb * zt, zt)]

    def ship_field(j, carry):
        k = my_yb * nyb + j

        @pl.when(k == me)
        def keep():
            pltpu.make_async_copy(nfb.at[j], nf_home, sem_rn).start()

        @pl.when(k != me)
        def send():
            remote(nfb.at[j], nf_home, sem_sn, sem_rn, (sp, k)).start()

        return carry

    lax.fori_loop(0, nyb, ship_field, 0)

    def drain(ref, sem):
        pltpu.make_async_copy(ref, ref, sem).wait()

    drain(nf_hbm, sem_rn)
    drain(out_hbm, sem_r2)
    drain(qext.at[:, pl.ds(0, 2)], sem_hqs)
    drain(send1.at[0, pl.ds(0, groups - 1)], sem_s1)
    drain(send1.at[1, pl.ds(0, groups - 1)], sem_s1)
    drain(precv.at[pl.ds(0, groups - 1)], sem_sp)
    drain(ext.at[pl.ds(0, 2), pl.ds(1, yt)], sem_hzs)
    drain(ext.at[0, pl.ds(0, 4)], sem_hys)
    drain(send2.at[0, pl.ds(0, groups - 1)], sem_s2)
    drain(send2.at[1, pl.ds(0, groups - 1)], sem_s2)

    sent_self = my_zb == my_yb

    @pl.when(sent_self)
    def drain_most():
        drain(nfb.at[pl.ds(0, nyb - 1)], sem_sn)

    @pl.when(jnp.logical_not(sent_self))
    def drain_all():
        drain(nfb, sem_sn)


def per_device(q_init, partner, field, orientations, orient_weight, rotation):
    count, nz, ny, nx = q_init.shape
    no = orientations.shape[1]
    nzb, nyb = nz // ZT, ny // YT
    groups = lax.axis_size("orient")
    spaces = lax.axis_size("space")
    dims = (spaces, groups, nzb, nyb, count, nz, ny, nx)
    pairs = ny // groups
    along = jnp.broadcast_to(orientations[:, :, None], (3, no, nx))
    hbm = pl.BlockSpec(memory_space=pl.ANY)
    vmem = pl.BlockSpec(memory_space=pltpu.VMEM)
    smem = pl.BlockSpec(memory_space=pltpu.SMEM)
    dma = pltpu.SemaphoreType.DMA
    return pl.pallas_call(
        functools.partial(whole_kernel, dims),
        in_specs=[hbm, hbm, hbm, vmem, vmem, smem, smem],
        out_specs=[hbm, hbm],
        out_shape=[
            jax.ShapeDtypeStruct((count, nz, ny, nx), BF16),
            jax.ShapeDtypeStruct((6, nz, pairs, nx), F32),
        ],
        scratch_shapes=[
            pltpu.VMEM((count, nz + 2, ny, nx), BF16),
            pltpu.VMEM((6, nz, ny, nx), BF16),
            pltpu.VMEM((ZT, groups, count, YT, nx), BF16),
            pltpu.VMEM((ZT, groups, count, YT, nx), BF16),
            pltpu.VMEM((ZT + 2, YT + 2, no, nx), BF16),
            pltpu.VMEM((no * YT, nx), F32),
            pltpu.VMEM((groups, count, ZT, YT, nx), BF16),
            pltpu.VMEM((ZT, groups, count, YT, nx), BF16),
            pltpu.VMEM((nyb, 6, ZT, pairs, nx), F32),
            pltpu.VMEM((4, no, nx), F32),
            pltpu.VMEM((no, nx), BF16),
            pltpu.VMEM((ZT * YT * 8, nx), F32),
            pltpu.VMEM((YT, nx), F32),
            dma((2,)),
            dma((2,)),
            dma(()),
            dma((ZT,)),
            dma(()),
            dma(()),
            dma(()),
            dma((2, CHUNKS)),
            dma(()),
            dma((2, ZT)),
            dma(()),
            dma(()),
            dma(()),
            dma(()),
            dma(()),
        ],
        compiler_params=pltpu.CompilerParams(
            collective_id=0, has_side_effects=True, vmem_limit_bytes=52 << 20
        ),
        name="whole",
    )(q_init, partner, field, along, rotation, orientations, orient_weight)


def solution(mesh):
    in_specs = (
        P("orient", "space", None, None),
        P("orient", "space", None, None),
        P(None, "space", None, None),
        P(),
        P(),
        P(),
    )
    out_specs = (P("orient", "space", None, None), P(None, "space", "orient", None))
    return jax.shard_map(
        per_device, mesh=mesh, in_specs=in_specs, out_specs=out_specs, check_vma=False
    )
```

```python
import functools

import jax
import jax.numpy as jnp
from jax import lax
from jax.experimental import pallas as pl
from jax.experimental.pallas import tpu as pltpu
from jax.sharding import PartitionSpec as P

step_length = 0.3
relax_rate = 0.5
coupling = 8.0

F32 = jnp.float32
BF16 = jnp.bfloat16
MESH = pl.DeviceIdType.MESH
ZT = 2
YT = 16
CHUNKS = 4
EARLY = 13


def whole_kernel(
    dims,
    q_hbm,
    part_hbm,
    w_hbm,
    rot_hbm,
    dirs_hbm,
    weight_hbm,
    out_hbm,
    nf_hbm,
    rot_ref,
    dirs_row,
    dirs,
    weight,
    ub_ref,
    qext,
    wv,
    send1,
    recv1,
    ext,
    wide,
    precv,
    send2,
    nfb,
    cf,
    ft3,
    wown,
    acc,
    sem_in,
    sem_hq,
    sem_hqs,
    sem_r1,
    sem_s1,
    sem_rp,
    sem_sp,
    sem_hz,
    sem_hzs,
    sem_hy,
    sem_hys,
    sem_r2,
    sem_s2,
    sem_rn,
    sem_sn,
):
    spaces, groups, nzb, nyb, count, nz, ny, nx = dims
    no = groups * count
    zt, yt = ZT, YT
    per = yt // CHUNKS
    me = lax.axis_index("orient")
    sp = lax.axis_index("space")
    my_zb = me // nyb
    my_yb = me % nyb
    sp_next = lax.rem(sp + 1, spaces)
    sp_prev = lax.rem(sp + spaces - 1, spaces)
    up = my_zb + 1
    z_next = (lax.rem(sp + up // nzb, spaces), lax.rem(up, nzb) * nyb + my_yb)
    down = my_zb + nzb - 1
    z_prev = (
        lax.rem(sp + spaces - 1 + down // nzb, spaces),
        lax.rem(down, nzb) * nyb + my_yb,
    )
    y_next = (sp, my_zb * nyb + lax.rem(my_yb + 1, nyb))
    y_prev = (sp, my_zb * nyb + lax.rem(my_yb + nyb - 1, nyb))

    load_q = pltpu.make_async_copy(q_hbm, qext.at[:, pl.ds(1, nz)], sem_in.at[0])
    load_w = pltpu.make_async_copy(w_hbm, wv, sem_in.at[1])
    loads = [
        pltpu.make_async_copy(dirs_hbm, dirs, sem_in.at[2]),
        pltpu.make_async_copy(dirs_hbm, dirs_row, sem_in.at[3]),
        pltpu.make_async_copy(weight_hbm, weight, sem_in.at[4]),
        pltpu.make_async_copy(rot_hbm, rot_ref, sem_in.at[5]),
    ]
    load_q.start()
    load_w.start()
    for load in loads:
        load.start()

    barrier = pltpu.get_barrier_semaphore()

    def greet(i, carry):
        peer = lax.rem(me + i, groups)
        pl.semaphore_signal(barrier, 1, device_id=(sp, peer), device_id_type=MESH)
        return carry

    for target in (z_next, z_prev, (sp_next, me), (sp_prev, me)):
        pl.semaphore_signal(barrier, 1, device_id=target, device_id_type=MESH)
    lax.fori_loop(1, groups, greet, 0)
    pl.semaphore_wait(barrier, groups + 3)

    def remote(src, dst, ssem, rsem, target):
        return pltpu.make_async_remote_copy(
            src_ref=src,
            dst_ref=dst,
            send_sem=ssem,
            recv_sem=rsem,
            device_id=target,
            device_id_type=MESH,
        )

    remote(
        q_hbm.at[:, pl.ds(nz - 1, 1)], qext.at[:, pl.ds(0, 1)], sem_hqs, sem_hq.at[0], (sp_next, me)
    ).start()
    remote(
        q_hbm.at[:, pl.ds(0, 1)], qext.at[:, pl.ds(nz + 1, 1)], sem_hqs, sem_hq.at[1], (sp_prev, me)
    ).start()

    def part_block(d):
        return part_hbm.at[:, pl.ds((d // nyb) * zt, zt), pl.ds(lax.rem(d, nyb) * yt, yt)]

    def ship_part(i, carry):
        d = lax.rem(me + i, groups)
        remote(part_block(d), precv.at[me], sem_sp, sem_rp, (sp, d)).start()
        return carry

    lax.fori_loop(1, EARLY, ship_part, 0)
    load_q.wait()
    load_w.wait()
    for load in loads:
        load.wait()

    for p in range(zt):

        def advect_plane(i, carry, p=p):
            zb = lax.rem(my_zb + 1 + i, nzb)
            z = zb * zt + p
            if p == 0:

                @pl.when(zb == 0)
                def low_halo():
                    pltpu.make_async_copy(
                        qext.at[:, pl.ds(0, 1)], qext.at[:, pl.ds(0, 1)], sem_hq.at[0]
                    ).wait()

            if p == zt - 1:

                @pl.when(zb == nzb - 1)
                def high_halo():
                    pltpu.make_async_copy(
                        qext.at[:, pl.ds(nz + 1, 1)], qext.at[:, pl.ds(nz + 1, 1)], sem_hq.at[1]
                    ).wait()

            planes = [wv[c, z].astype(F32) for c in range(6)]
            for o in range(count):
                ux = dirs[0, me * count + o]
                uy = dirs[1, me * count + o]
                uz = dirs[2, me * count + o]
                ax = step_length * jnp.maximum(ux, -ux)
                ay = step_length * jnp.maximum(uy, -uy)
                az = step_length * jnp.maximum(uz, -uz)
                terms = (ux * ux, uy * uy, uz * uz, 2.0 * ux * uy, 2.0 * ux * uz, 2.0 * uy * uz)
                f = qext[o, z + 1].astype(F32)
                below = qext[o, z].astype(F32)
                above = qext[o, z + 2].astype(F32)
                up_x = jnp.where(ux > 0.0, pltpu.roll(f, 1, 1), pltpu.roll(f, nx - 1, 1))
                up_y = jnp.where(uy > 0.0, pltpu.roll(f, 1, 0), pltpu.roll(f, ny - 1, 0))
                up_z = jnp.where(uz > 0.0, below, above)
                moved = f * (1.0 - (ax + ay + az)) + ax * up_x + ay * up_y + az * up_z
                power = (-step_length * terms[0]) * planes[0]
                for c in range(1, 6):
                    power = power + (-step_length * terms[c]) * planes[c]
                res = (moved * jnp.exp(power)).astype(BF16)
                for yb in range(nyb):
                    send1[p, zb * nyb + yb, o] = res[yb * yt : (yb + 1) * yt]

            def ship(j, inner):
                yb = lax.rem(my_yb + 1 + j, nyb)
                d = zb * nyb + yb

                @pl.when(d == me)
                def keep():
                    pltpu.make_async_copy(send1.at[p, d], recv1.at[p, me], sem_r1.at[p]).start()

                @pl.when(d != me)
                def send():
                    remote(
                        send1.at[p, d], recv1.at[p, me], sem_s1, sem_r1.at[p], (sp, d)
                    ).start()

                return inner

            lax.fori_loop(0, nyb, ship, 0)
            return carry

        lax.fori_loop(0, nzb, advect_plane, 0)

    lax.fori_loop(EARLY, groups, ship_part, 0)
    pltpu.make_async_copy(part_block(me), precv.at[me], sem_rp).start()

    diagonal = lax.broadcasted_iota(jnp.int32, (no, no), 0) == lax.broadcasted_iota(
        jnp.int32, (no, no), 1
    )
    for a in range(3):
        spread = jnp.where(diagonal, jnp.broadcast_to(dirs_row[pl.ds(a, 1), :], (no, no)), 0.0)
        ub_ref[a] = jnp.broadcast_to(jnp.sum(spread, axis=1, keepdims=True), (no, nx))
    ux = ub_ref[0]
    uy = ub_ref[1]
    uz = ub_ref[2]
    ax = step_length * jnp.abs(ux)
    ay = step_length * jnp.abs(uy)
    az = step_length * jnp.abs(uz)
    cf[0] = 1.0 - (ax + ay + az)
    cf[1] = ax
    cf[2] = ay
    cf[3] = az
    lane = lax.broadcasted_iota(jnp.int32, (no, nx), 1)
    terms = (ux * ux, uy * uy, uz * uz, 2.0 * ux * uy, 2.0 * ux * uz, 2.0 * uy * uz)
    packed = jnp.zeros((no, nx), F32)
    for c in range(6):
        value = -step_length * terms[c]
        high = value.astype(BF16).astype(F32)
        rest = value - high
        mid = rest.astype(BF16).astype(F32)
        low = rest - mid
        packed = jnp.where(lane == c, high, packed)
        packed = jnp.where(lane == 8 + c, mid, packed)
        packed = jnp.where(lane == 16 + c, low, packed)
    ft3[...] = packed.astype(BF16)

    wown[...] = jnp.zeros_like(wown)
    for p in range(zt):
        for c in range(6):
            block = wv[c, my_zb * zt + p, pl.ds(pl.multiple_of(my_yb * yt, yt), yt)]
            wown[pl.ds(p * yt * 8 + c, yt, stride=8), :] = block.astype(F32)

    for p in range(zt):
        pltpu.make_async_copy(recv1.at[p], recv1.at[p], sem_r1.at[p]).wait()

        def widen(s, carry, p=p):
            rows = count * yt
            wide[pl.ds(pl.multiple_of(s * rows, rows), rows), :] = (
                recv1[p, s].astype(F32).reshape(rows, nx)
            )
            return carry

        lax.fori_loop(0, groups, widen, 0, unroll=4)
        for chunk in range(CHUNKS):

            def turn(k, carry, p=p, chunk=chunk):
                y = chunk * per + k
                tile = wide[pl.ds(y, no, stride=yt), :].astype(BF16)
                turned = jnp.dot(rot_ref[...], tile, preferred_element_type=F32)
                ext[p + 1, y + 1] = turned.astype(BF16)
                return carry

            lax.fori_loop(0, per, turn, 0, unroll=2)
            rows = pl.ds(1 + chunk * per, per)
            if p == 0:
                remote(
                    ext.at[1, rows], ext.at[zt + 1, rows], sem_hzs, sem_hz.at[1, chunk], z_prev
                ).start()
            if p == zt - 1:
                remote(
                    ext.at[zt, rows], ext.at[0, rows], sem_hzs, sem_hz.at[0, chunk], z_next
                ).start()
            if chunk == 0:
                remote(
                    ext.at[p + 1, pl.ds(1, 1)],
                    ext.at[p + 1, pl.ds(yt + 1, 1)],
                    sem_hys,
                    sem_hy.at[1, p],
                    y_prev,
                ).start()
            if chunk == CHUNKS - 1:
                remote(
                    ext.at[p + 1, pl.ds(yt, 1)],
                    ext.at[p + 1, pl.ds(0, 1)],
                    sem_hys,
                    sem_hy.at[0, p],
                    y_next,
                ).start()

    for p in reversed(range(zt)):
        for side, row in ((0, 0), (1, yt + 1)):
            face = ext.at[p + 1, pl.ds(row, 1)]
            pltpu.make_async_copy(face, face, sem_hy.at[side, p]).wait()
        for chunk in range(CHUNKS):
            rows = pl.ds(1 + chunk * per, per)
            if p == zt - 1:
                face = ext.at[zt + 1, rows]
                pltpu.make_async_copy(face, face, sem_hz.at[1, chunk]).wait()
            if p == 0:
                face = ext.at[0, rows]
                pltpu.make_async_copy(face, face, sem_hz.at[0, chunk]).wait()

            def step(k, carry, p=p, chunk=chunk):
                y = chunk * per + k
                f = ext[p + 1, y + 1].astype(F32)
                up_x = jnp.where(ub_ref[0] > 0.0, pltpu.roll(f, 1, 1), pltpu.roll(f, nx - 1, 1))
                up_y = jnp.where(
                    ub_ref[1] > 0.0, ext[p + 1, y].astype(F32), ext[p + 1, y + 2].astype(F32)
                )
                up_z = jnp.where(
                    ub_ref[2] > 0.0, ext[p, y + 1].astype(F32), ext[p + 2, y + 1].astype(F32)
                )
                moved = f * cf[0] + cf[1] * up_x + cf[2] * up_y + cf[3] * up_z
                w8 = wown[pl.ds(pl.multiple_of((p * yt + y) * 8, 8), 8), :]
                w24 = jnp.concatenate([w8, w8, w8], axis=0).astype(BF16)
                power = jnp.dot(ft3[:, :24], w24, preferred_element_type=F32)
                adv = (moved * jnp.exp(power)).astype(BF16)
                turned = jnp.dot(rot_ref[...], adv, preferred_element_type=F32)
                wide[pl.ds(y, no, stride=yt), :] = turned
                return carry

            lax.fori_loop(0, per, step, 0)

        def ship_home(i, carry, p=p):
            d = lax.rem(me + 1 + i, groups)
            rows = count * yt
            block = wide[pl.ds(pl.multiple_of(d * rows, rows), rows), :]
            send2[p, d] = block.astype(BF16).reshape(count, yt, nx)
            home = out_hbm.at[:, my_zb * zt + p, pl.ds(pl.multiple_of(my_yb * yt, yt), yt)]

            @pl.when(d == me)
            def keep():
                pltpu.make_async_copy(send2.at[p, d], home, sem_r2).start()

            @pl.when(d != me)
            def send():
                remote(send2.at[p, d], home, sem_s2, sem_r2, (sp, d)).start()

            return carry

        lax.fori_loop(0, groups, ship_home, 0)

    pltpu.make_async_copy(precv, precv, sem_rp).wait()
    for p in range(zt):

        def add_terms(d, sums, p=p):
            sums = list(sums)
            for o in range(count):
                gx = dirs[0, d * count + o]
                gy = dirs[1, d * count + o]
                gz = dirs[2, d * count + o]
                gw = weight[d * count + o]
                third = 1.0 / 3.0
                factors = (
                    (gx * gx - third) * gw,
                    (gy * gy - third) * gw,
                    (gz * gz - third) * gw,
                    gx * gy * gw,
                    gx * gz * gw,
                    gy * gz * gw,
                )
                prod = send2[p, d, o].astype(F32) * precv[d, o, p].astype(F32)
                for c in range(6):
                    sums[c] = sums[c] + factors[c] * prod
            return tuple(sums)

        sums = lax.fori_loop(
            0, groups, add_terms, tuple(jnp.zeros((yt, nx), F32) for c in range(6))
        )
        for c in range(6):
            old = wv[c, my_zb * zt + p, pl.ds(pl.multiple_of(my_yb * yt, yt), yt)].astype(F32)
            acc[...] = (1.0 - relax_rate) * old + relax_rate * coupling * sums[c]
            for j in range(nyb):
                nfb[j, c, p] = acc[pl.ds(2 * j, 2), :]

    nf_home = nf_hbm.at[:, pl.ds(my_zb * zt, zt)]

    def ship_field(j, carry):
        k = my_yb * nyb + j

        @pl.when(k == me)
        def keep():
            pltpu.make_async_copy(nfb.at[j], nf_home, sem_rn).start()

        @pl.when(k != me)
        def send():
            remote(nfb.at[j], nf_home, sem_sn, sem_rn, (sp, k)).start()

        return carry

    lax.fori_loop(0, nyb, ship_field, 0)

    def drain(ref, sem):
        pltpu.make_async_copy(ref, ref, sem).wait()

    drain(nf_hbm, sem_rn)
    drain(out_hbm, sem_r2)
    drain(qext.at[:, pl.ds(0, 2)], sem_hqs)
    drain(send1.at[0, pl.ds(0, groups - 1)], sem_s1)
    drain(send1.at[1, pl.ds(0, groups - 1)], sem_s1)
    drain(precv.at[pl.ds(0, groups - 1)], sem_sp)
    drain(ext.at[pl.ds(0, 2), pl.ds(1, yt)], sem_hzs)
    drain(ext.at[0, pl.ds(0, 4)], sem_hys)
    drain(send2.at[0, pl.ds(0, groups - 1)], sem_s2)
    drain(send2.at[1, pl.ds(0, groups - 1)], sem_s2)

    sent_self = my_zb == my_yb

    @pl.when(sent_self)
    def drain_most():
        drain(nfb.at[pl.ds(0, nyb - 1)], sem_sn)

    @pl.when(jnp.logical_not(sent_self))
    def drain_all():
        drain(nfb, sem_sn)


def per_device(q_init, partner, field, orientations, orient_weight, rotation):
    count, nz, ny, nx = q_init.shape
    no = orientations.shape[1]
    nzb, nyb = nz // ZT, ny // YT
    groups = lax.axis_size("orient")
    spaces = lax.axis_size("space")
    dims = (spaces, groups, nzb, nyb, count, nz, ny, nx)
    pairs = ny // groups
    hbm = pl.BlockSpec(memory_space=pltpu.HBM)
    anywhere = pl.BlockSpec(memory_space=pltpu.VMEM)
    dma = pltpu.SemaphoreType.DMA
    return pl.pallas_call(
        functools.partial(whole_kernel, dims),
        in_specs=[hbm] * 6,
        out_specs=[anywhere, anywhere],
        out_shape=[
            jax.ShapeDtypeStruct((count, nz, ny, nx), BF16),
            jax.ShapeDtypeStruct((6, nz, pairs, nx), F32),
        ],
        scratch_shapes=[
            pltpu.VMEM((no, no), BF16),
            pltpu.VMEM((3, no), F32),
            pltpu.SMEM((3, no), F32),
            pltpu.SMEM((no,), F32),
            pltpu.VMEM((3, no, nx), F32),
            pltpu.VMEM((count, nz + 2, ny, nx), BF16),
            pltpu.VMEM((6, nz, ny, nx), BF16),
            pltpu.VMEM((ZT, groups, count, YT, nx), BF16),
            pltpu.VMEM((ZT, groups, count, YT, nx), BF16),
            pltpu.VMEM((ZT + 2, YT + 2, no, nx), BF16),
            pltpu.VMEM((no * YT, nx), F32),
            pltpu.VMEM((groups, count, ZT, YT, nx), BF16),
            pltpu.VMEM((ZT, groups, count, YT, nx), BF16),
            pltpu.VMEM((nyb, 6, ZT, pairs, nx), F32),
            pltpu.VMEM((4, no, nx), F32),
            pltpu.VMEM((no, nx), BF16),
            pltpu.VMEM((ZT * YT * 8, nx), F32),
            pltpu.VMEM((YT, nx), F32),
            dma((6,)),
            dma((2,)),
            dma(()),
            dma((ZT,)),
            dma(()),
            dma(()),
            dma(()),
            dma((2, CHUNKS)),
            dma(()),
            dma((2, ZT)),
            dma(()),
            dma(()),
            dma(()),
            dma(()),
            dma(()),
        ],
        compiler_params=pltpu.CompilerParams(
            collective_id=0, has_side_effects=True, vmem_limit_bytes=40 << 20
        ),
        name="whole",
    )(
        *[
            pltpu.with_memory_space_constraint(x, pltpu.HBM)
            for x in (q_init, partner, field, rotation, orientations, orient_weight)
        ]
    )


def solution(mesh):
    in_specs = (
        P("orient", "space", None, None),
        P("orient", "space", None, None),
        P(None, "space", None, None),
        P(),
        P(),
        P(),
    )
    out_specs = (P("orient", "space", None, None), P(None, "space", "orient", None))
    return jax.shard_map(
        per_device, mesh=mesh, in_specs=in_specs, out_specs=out_specs, check_vma=False
    )
```

```python
import functools

import jax
import jax.numpy as jnp
from jax import lax
from jax.experimental import pallas as pl
from jax.experimental.pallas import tpu as pltpu
from jax.sharding import PartitionSpec as P

step_length = 0.3
relax_rate = 0.5
coupling = 8.0

F32 = jnp.float32
BF16 = jnp.bfloat16
MESH = pl.DeviceIdType.MESH
ZT = 2
YT = 16
CHUNKS = 4
EARLY = 0
LATE = 0
PART_ORDER = (4, 3, 5, 2, 6, 1, 7, 0)
Z_ORDER = (4, 3, 5, 2, 6, 1, 7, 0)
XY_ORDER = (4, 3, 5, 2, 6, 1, 7, 0)


def whole_kernel(
    dims,
    q_hbm,
    part_hbm,
    w_hbm,
    rot_hbm,
    dirs_hbm,
    weight_hbm,
    out_hbm,
    nf_hbm,
    rot_ref,
    dirs_row,
    dirs,
    weight,
    ub_ref,
    qext,
    wv,
    send1,
    recv1,
    ext,
    wide,
    pmid,
    send2,
    mid,
    pt,
    rs,
    tt,
    nfb,
    cf,
    ft3,
    wown,
    sem_in,
    sem_hq,
    sem_hqs,
    sem_r1,
    sem_s1,
    sem_rp,
    sem_sp,
    sem_hz,
    sem_hzs,
    sem_hy,
    sem_hys,
    sem_rm,
    sem_sm,
    sem_ro,
    sem_so,
    sem_rt,
    sem_st,
    sem_rn,
    sem_sn,
):
    spaces, groups, nzb, nyb, count, nz, ny, nx = dims
    no = groups * count
    zt, yt = ZT, YT
    per = yt // CHUNKS
    half = yt // 2
    me = lax.axis_index("orient")
    sp = lax.axis_index("space")
    my_zb = me // nyb
    my_yb = me % nyb
    sp_next = lax.rem(sp + 1, spaces)
    sp_prev = lax.rem(sp + spaces - 1, spaces)
    up = my_zb + 1
    z_next = (lax.rem(sp + up // nzb, spaces), lax.rem(up, nzb) * nyb + my_yb)
    down = my_zb + nzb - 1
    z_prev = (
        lax.rem(sp + spaces - 1 + down // nzb, spaces),
        lax.rem(down, nzb) * nyb + my_yb,
    )
    y_next = (sp, my_zb * nyb + lax.rem(my_yb + 1, nyb))
    y_prev = (sp, my_zb * nyb + lax.rem(my_yb + nyb - 1, nyb))

    load_q = pltpu.make_async_copy(q_hbm, qext.at[:, pl.ds(1, nz)], sem_in.at[0])
    load_w = pltpu.make_async_copy(w_hbm, wv, sem_in.at[1])
    loads = [
        pltpu.make_async_copy(dirs_hbm, dirs, sem_in.at[2]),
        pltpu.make_async_copy(dirs_hbm, dirs_row, sem_in.at[3]),
        pltpu.make_async_copy(weight_hbm, weight, sem_in.at[4]),
        pltpu.make_async_copy(rot_hbm, rot_ref, sem_in.at[5]),
    ]
    load_q.start()
    load_w.start()
    for load in loads:
        load.start()

    barrier = pltpu.get_barrier_semaphore()

    def greet(i, carry):
        peer = lax.rem(me + i, groups)
        pl.semaphore_signal(barrier, 1, device_id=(sp, peer), device_id_type=MESH)
        return carry

    for target in (z_next, z_prev, (sp_next, me), (sp_prev, me)):
        pl.semaphore_signal(barrier, 1, device_id=target, device_id_type=MESH)
    lax.fori_loop(1, groups, greet, 0)
    pl.semaphore_wait(barrier, groups + 3)

    def remote(src, dst, ssem, rsem, target):
        return pltpu.make_async_remote_copy(
            src_ref=src,
            dst_ref=dst,
            send_sem=ssem,
            recv_sem=rsem,
            device_id=target,
            device_id_type=MESH,
        )

    remote(
        q_hbm.at[:, pl.ds(nz - 1, 1)], qext.at[:, pl.ds(0, 1)], sem_hqs, sem_hq.at[0], (sp_next, me)
    ).start()
    remote(
        q_hbm.at[:, pl.ds(0, 1)], qext.at[:, pl.ds(nz + 1, 1)], sem_hqs, sem_hq.at[1], (sp_prev, me)
    ).start()

    def ship_part(i):
        xy = lax.rem(my_zb + i, nzb)
        slot = (nzb - i) % nzb
        src = part_hbm.at[:, pl.ds(xy * zt, zt)]
        if i == 0:
            pltpu.make_async_copy(src, pmid.at[slot], sem_rp).start()
        else:
            remote(src, pmid.at[slot], sem_sp, sem_rp, (sp, xy * nyb + my_yb)).start()

    for i in PART_ORDER[:EARLY]:
        ship_part(i)
    load_q.wait()
    load_w.wait()
    for load in loads:
        load.wait()

    for p in range(zt):

        def advect_plane(i, carry, p=p):
            zb = lax.rem(my_zb + 1 + i, nzb)
            z = zb * zt + p
            if p == 0:

                @pl.when(zb == 0)
                def low_halo():
                    pltpu.make_async_copy(
                        qext.at[:, pl.ds(0, 1)], qext.at[:, pl.ds(0, 1)], sem_hq.at[0]
                    ).wait()

            if p == zt - 1:

                @pl.when(zb == nzb - 1)
                def high_halo():
                    pltpu.make_async_copy(
                        qext.at[:, pl.ds(nz + 1, 1)], qext.at[:, pl.ds(nz + 1, 1)], sem_hq.at[1]
                    ).wait()

            planes = [wv[c, z].astype(F32) for c in range(6)]
            for o in range(count):
                ux = dirs[0, me * count + o]
                uy = dirs[1, me * count + o]
                uz = dirs[2, me * count + o]
                ax = step_length * jnp.maximum(ux, -ux)
                ay = step_length * jnp.maximum(uy, -uy)
                az = step_length * jnp.maximum(uz, -uz)
                terms = (ux * ux, uy * uy, uz * uz, 2.0 * ux * uy, 2.0 * ux * uz, 2.0 * uy * uz)
                f = qext[o, z + 1].astype(F32)
                below = qext[o, z].astype(F32)
                above = qext[o, z + 2].astype(F32)
                up_x = jnp.where(ux > 0.0, pltpu.roll(f, 1, 1), pltpu.roll(f, nx - 1, 1))
                up_y = jnp.where(uy > 0.0, pltpu.roll(f, 1, 0), pltpu.roll(f, ny - 1, 0))
                up_z = jnp.where(uz > 0.0, below, above)
                moved = f * (1.0 - (ax + ay + az)) + ax * up_x + ay * up_y + az * up_z
                power = (-step_length * terms[0]) * planes[0]
                for c in range(1, 6):
                    power = power + (-step_length * terms[c]) * planes[c]
                res = (moved * jnp.exp(power)).astype(BF16)
                for yb in range(nyb):
                    send1[p, zb * nyb + yb, o] = res[yb * yt : (yb + 1) * yt]

            def ship(j, inner):
                yb = lax.rem(my_yb + 1 + j, nyb)
                d = zb * nyb + yb

                @pl.when(d == me)
                def keep():
                    pltpu.make_async_copy(send1.at[p, d], recv1.at[p, me], sem_r1.at[p]).start()

                @pl.when(d != me)
                def send():
                    remote(
                        send1.at[p, d], recv1.at[p, me], sem_s1, sem_r1.at[p], (sp, d)
                    ).start()

                return inner

            lax.fori_loop(0, nyb, ship, 0)
            return carry

        lax.fori_loop(0, nzb, advect_plane, 0)

    for i in PART_ORDER[EARLY:LATE]:
        ship_part(i)

    diagonal = lax.broadcasted_iota(jnp.int32, (no, no), 0) == lax.broadcasted_iota(
        jnp.int32, (no, no), 1
    )
    for a in range(3):
        spread = jnp.where(diagonal, jnp.broadcast_to(dirs_row[pl.ds(a, 1), :], (no, no)), 0.0)
        ub_ref[a] = jnp.broadcast_to(jnp.sum(spread, axis=1, keepdims=True), (no, nx))
    ux = ub_ref[0]
    uy = ub_ref[1]
    uz = ub_ref[2]
    ax = step_length * jnp.abs(ux)
    ay = step_length * jnp.abs(uy)
    az = step_length * jnp.abs(uz)
    cf[0] = 1.0 - (ax + ay + az)
    cf[1] = ax
    cf[2] = ay
    cf[3] = az
    lane = lax.broadcasted_iota(jnp.int32, (no, nx), 1)
    terms = (ux * ux, uy * uy, uz * uz, 2.0 * ux * uy, 2.0 * ux * uz, 2.0 * uy * uz)
    packed = jnp.zeros((no, nx), F32)
    for c in range(6):
        value = -step_length * terms[c]
        high = value.astype(BF16).astype(F32)
        rest = value - high
        middle = rest.astype(BF16).astype(F32)
        low = rest - middle
        packed = jnp.where(lane == c, high, packed)
        packed = jnp.where(lane == 8 + c, middle, packed)
        packed = jnp.where(lane == 16 + c, low, packed)
    ft3[...] = packed.astype(BF16)

    wown[...] = jnp.zeros_like(wown)
    for p in range(zt):
        for c in range(6):
            block = wv[c, my_zb * zt + p, pl.ds(pl.multiple_of(my_yb * yt, yt), yt)]
            wown[pl.ds(p * yt * 8 + c, yt, stride=8), :] = block.astype(F32)

    for p in range(zt):
        pltpu.make_async_copy(recv1.at[p], recv1.at[p], sem_r1.at[p]).wait()

        def widen(s, carry, p=p):
            rows = count * yt
            wide[pl.ds(pl.multiple_of(s * rows, rows), rows), :] = (
                recv1[p, s].astype(F32).reshape(rows, nx)
            )
            return carry

        lax.fori_loop(0, groups, widen, 0, unroll=4)
        for chunk in range(CHUNKS):

            def turn(k, carry, p=p, chunk=chunk):
                y = chunk * per + k
                tile = wide[pl.ds(y, no, stride=yt), :].astype(BF16)
                turned = jnp.dot(rot_ref[...], tile, preferred_element_type=F32)
                ext[p + 1, y + 1] = turned.astype(BF16)
                return carry

            lax.fori_loop(0, per, turn, 0, unroll=2)
            rows = pl.ds(1 + chunk * per, per)
            if p == 0:
                remote(
                    ext.at[1, rows], ext.at[zt + 1, rows], sem_hzs, sem_hz.at[1, chunk], z_prev
                ).start()
            if p == zt - 1:
                remote(
                    ext.at[zt, rows], ext.at[0, rows], sem_hzs, sem_hz.at[0, chunk], z_next
                ).start()
            if chunk == 0:
                remote(
                    ext.at[p + 1, pl.ds(1, 1)],
                    ext.at[p + 1, pl.ds(yt + 1, 1)],
                    sem_hys,
                    sem_hy.at[1, p],
                    y_prev,
                ).start()
            if chunk == CHUNKS - 1:
                remote(
                    ext.at[p + 1, pl.ds(yt, 1)],
                    ext.at[p + 1, pl.ds(0, 1)],
                    sem_hys,
                    sem_hy.at[0, p],
                    y_next,
                ).start()

    for i in PART_ORDER[LATE:]:
        ship_part(i)

    def factor(i, carry):
        o = (lax.rem(my_zb + i // count, nzb) * nyb + my_yb) * count + lax.rem(i, count)
        gx = dirs[0, o]
        gy = dirs[1, o]
        gz = dirs[2, o]
        gw = weight[o]
        third = 1.0 / 3.0
        tt[0, i] = (gx * gx - third) * gw
        tt[1, i] = (gy * gy - third) * gw
        tt[2, i] = (gz * gz - third) * gw
        tt[3, i] = gx * gy * gw
        tt[4, i] = gx * gz * gw
        tt[5, i] = gy * gz * gw
        return carry

    lax.fori_loop(0, nzb * count, factor, 0)

    def await_copy(ref, sem):
        pltpu.make_async_copy(ref, ref, sem).wait()

    def second_step(p, h):
        face = ext.at[p + 1, pl.ds((yt + 1) * h, 1)]
        await_copy(face, sem_hy.at[h, p])
        for chunk in range(h * CHUNKS // 2, (h + 1) * CHUNKS // 2):
            rows = pl.ds(1 + chunk * per, per)
            if p == zt - 1:
                await_copy(ext.at[zt + 1, rows], sem_hz.at[1, chunk])
            if p == 0:
                await_copy(ext.at[0, rows], sem_hz.at[0, chunk])

            def step(k, carry, chunk=chunk):
                y = chunk * per + k
                f = ext[p + 1, y + 1].astype(F32)
                up_x = jnp.where(ub_ref[0] > 0.0, pltpu.roll(f, 1, 1), pltpu.roll(f, nx - 1, 1))
                up_y = jnp.where(
                    ub_ref[1] > 0.0, ext[p + 1, y].astype(F32), ext[p + 1, y + 2].astype(F32)
                )
                up_z = jnp.where(
                    ub_ref[2] > 0.0, ext[p, y + 1].astype(F32), ext[p + 2, y + 1].astype(F32)
                )
                moved = f * cf[0] + cf[1] * up_x + cf[2] * up_y + cf[3] * up_z
                w8 = wown[pl.ds(pl.multiple_of((p * yt + y) * 8, 8), 8), :]
                w24 = jnp.concatenate([w8, w8, w8], axis=0).astype(BF16)
                power = jnp.dot(ft3[:, :24], w24, preferred_element_type=F32)
                adv = (moved * jnp.exp(power)).astype(BF16)
                turned = jnp.dot(rot_ref[...], adv, preferred_element_type=F32)
                wide[pl.ds(y - h * half, no, stride=half), :] = turned
                return carry

            lax.fori_loop(0, per, step, 0)

        for i in Z_ORDER:
            zc = lax.rem(my_yb + i, nyb)

            def pack(r, carry, zc=zc):
                d = lax.rem(my_zb + r, nzb) * nyb + zc
                rows = count * half
                block = wide[pl.ds(pl.multiple_of(d * rows, rows), rows), :]
                send2[p, h, zc, r] = block.astype(BF16).reshape(count, half, nx)
                return carry

            lax.fori_loop(0, nzb, pack, 0, unroll=4)
            src = send2.at[p, h, zc]
            dst = mid.at[p, h, :, :, my_yb]
            if i == 0:
                pltpu.make_async_copy(src, dst, sem_rm.at[p, h]).start()
            else:
                remote(src, dst, sem_sm, sem_rm.at[p, h], (sp, my_zb * nyb + zc)).start()

    def pass_on(p, h):
        await_copy(mid.at[p, h], sem_rm.at[p, h])
        home = out_hbm.at[:, my_zb * zt + p, :, h]
        for r in XY_ORDER:
            src = mid.at[p, h, r]
            if r == 0:
                pltpu.make_async_copy(src, home, sem_ro).start()
            else:
                xy = lax.rem(my_zb + r, nzb)
                remote(src, home, sem_so, sem_ro, (sp, xy * nyb + my_yb)).start()
        for g in range(2):
            blocks = pl.ds(g * nyb // 2, nyb // 2)

            def add_terms(i, sums, blocks=blocks):
                r = i // count
                o = lax.rem(i, count)
                prod = mid[p, h, r, o, blocks].astype(F32) * pmid[r, o, p, blocks, h].astype(F32)
                return tuple(sums[c] + tt[c, i] * prod for c in range(6))

            zero = jnp.zeros((nyb // 2, half, nx), F32)
            sums = lax.fori_loop(0, nzb * count, add_terms, (zero,) * 6)
            for c in range(6):
                pt[p, h, blocks, c] = sums[c]
        for i in Z_ORDER:
            zc = lax.rem(my_yb + i, nyb)
            src = pt.at[p, h, zc]
            dst = rs.at[p, h, my_yb]
            if i == 0:
                pltpu.make_async_copy(src, dst, sem_rt.at[p, h]).start()
            else:
                remote(src, dst, sem_st, sem_rt.at[p, h], (sp, my_zb * nyb + zc)).start()

    nf_home = nf_hbm.at[:, pl.ds(my_zb * zt, zt)]
    each = nyb // 2

    def relax(p, h):
        await_copy(rs.at[p, h], sem_rt.at[p, h])
        for c in range(6):
            total = rs[p, h, 0, c]
            for s in range(1, nyb):
                total = total + rs[p, h, s, c]
            old = wv[c, my_zb * zt + p, pl.ds(pl.multiple_of(my_yb * yt, yt), yt)].astype(F32)
            old = old[h * half : (h + 1) * half]
            value = (1.0 - relax_rate) * old + relax_rate * coupling * total
            for j in range(each):
                nfb[h * each + j, c, p] = value[2 * j : 2 * j + 2]
        if p == 0:

            def ship_field(j, carry):
                k = my_yb * nyb + j

                @pl.when(k == me)
                def keep():
                    pltpu.make_async_copy(nfb.at[j], nf_home, sem_rn).start()

                @pl.when(k != me)
                def send():
                    remote(nfb.at[j], nf_home, sem_sn, sem_rn, (sp, k)).start()

                return carry

            lax.fori_loop(h * each, (h + 1) * each, ship_field, 0)

    second_step(1, 0)
    second_step(1, 1)
    second_step(0, 0)
    await_copy(pmid, sem_rp)
    pass_on(1, 0)
    second_step(0, 1)
    pass_on(1, 1)
    relax(1, 0)
    pass_on(0, 0)
    relax(1, 1)
    pass_on(0, 1)
    relax(0, 0)
    relax(0, 1)

    def drain(ref, sem):
        pltpu.make_async_copy(ref, ref, sem).wait()

    drain(nf_hbm, sem_rn)
    drain(out_hbm, sem_ro)
    drain(qext.at[:, pl.ds(0, 2)], sem_hqs)
    drain(send1.at[0, pl.ds(0, groups - 1)], sem_s1)
    drain(send1.at[1, pl.ds(0, groups - 1)], sem_s1)
    drain(pmid.at[pl.ds(0, nzb - 1)], sem_sp)
    drain(ext.at[pl.ds(0, 2), pl.ds(1, yt)], sem_hzs)
    drain(ext.at[0, pl.ds(0, 4)], sem_hys)
    drain(send2.at[:, :, pl.ds(0, nyb - 1)], sem_sm)
    drain(mid.at[:, :, pl.ds(0, nzb - 1)], sem_so)
    drain(pt.at[:, :, pl.ds(0, nyb - 1)], sem_st)

    sent_self = my_zb == my_yb

    @pl.when(sent_self)
    def drain_most():
        drain(nfb.at[pl.ds(0, nyb - 1)], sem_sn)

    @pl.when(jnp.logical_not(sent_self))
    def drain_all():
        drain(nfb, sem_sn)


def per_device(q_init, partner, field, orientations, orient_weight, rotation):
    count, nz, ny, nx = q_init.shape
    no = orientations.shape[1]
    nzb, nyb = nz // ZT, ny // YT
    groups = lax.axis_size("orient")
    spaces = lax.axis_size("space")
    dims = (spaces, groups, nzb, nyb, count, nz, ny, nx)
    pairs = ny // groups
    hbm = pl.BlockSpec(memory_space=pltpu.HBM)
    anywhere = pl.BlockSpec(memory_space=pltpu.VMEM)
    dma = pltpu.SemaphoreType.DMA
    part = partner.reshape(count, nz, nyb, 2, YT // 2, nx)
    out, new_field = pl.pallas_call(
        functools.partial(whole_kernel, dims),
        in_specs=[hbm] * 6,
        out_specs=[anywhere, anywhere],
        out_shape=[
            jax.ShapeDtypeStruct((count, nz, nyb, 2, YT // 2, nx), BF16),
            jax.ShapeDtypeStruct((6, nz, pairs, nx), F32),
        ],
        scratch_shapes=[
            pltpu.VMEM((no, no), BF16),
            pltpu.VMEM((3, no), F32),
            pltpu.SMEM((3, no), F32),
            pltpu.SMEM((no,), F32),
            pltpu.VMEM((3, no, nx), F32),
            pltpu.VMEM((count, nz + 2, ny, nx), BF16),
            pltpu.VMEM((6, nz, ny, nx), BF16),
            pltpu.VMEM((ZT, groups, count, YT, nx), BF16),
            pltpu.VMEM((ZT, groups, count, YT, nx), BF16),
            pltpu.VMEM((ZT + 2, YT + 2, no, nx), BF16),
            pltpu.VMEM((no * YT, nx), F32),
            pltpu.VMEM((nzb, count, ZT, nyb, 2, YT // 2, nx), BF16),
            pltpu.VMEM((ZT, 2, nyb, nzb, count, YT // 2, nx), BF16),
            pltpu.VMEM((ZT, 2, nzb, count, nyb, YT // 2, nx), BF16),
            pltpu.VMEM((ZT, 2, nyb, 6, YT // 2, nx), F32),
            pltpu.VMEM((ZT, 2, nyb, 6, YT // 2, nx), F32),
            pltpu.SMEM((6, nzb * count), F32),
            pltpu.VMEM((nyb, 6, ZT, pairs, nx), F32),
            pltpu.VMEM((4, no, nx), F32),
            pltpu.VMEM((no, nx), BF16),
            pltpu.VMEM((ZT * YT * 8, nx), F32),
            dma((6,)),
            dma((2,)),
            dma(()),
            dma((ZT,)),
            dma(()),
            dma(()),
            dma(()),
            dma((2, CHUNKS)),
            dma(()),
            dma((2, ZT)),
            dma(()),
            dma((ZT, 2)),
            dma(()),
            dma(()),
            dma(()),
            dma((ZT, 2)),
            dma(()),
            dma(()),
            dma(()),
        ],
        compiler_params=pltpu.CompilerParams(
            collective_id=0, has_side_effects=True, vmem_limit_bytes=40 << 20
        ),
        name="whole",
    )(
        *[
            pltpu.with_memory_space_constraint(x, pltpu.HBM)
            for x in (q_init, part, field, rotation, orientations, orient_weight)
        ]
    )
    return out.reshape(count, nz, ny, nx), new_field


def solution(mesh):
    in_specs = (
        P("orient", "space", None, None),
        P("orient", "space", None, None),
        P(None, "space", None, None),
        P(),
        P(),
        P(),
    )
    out_specs = (P("orient", "space", None, None), P(None, "space", "orient", None))
    return jax.shard_map(
        per_device, mesh=mesh, in_specs=in_specs, out_specs=out_specs, check_vma=False
    )
```

```python
import functools

import jax
import jax.numpy as jnp
from jax import lax
from jax.experimental import pallas as pl
from jax.experimental.pallas import tpu as pltpu
from jax.sharding import PartitionSpec as P

step_length = 0.3
relax_rate = 0.5
coupling = 8.0

F32 = jnp.float32
BF16 = jnp.bfloat16
MESH = pl.DeviceIdType.MESH
ZT = 2
YT = 16
CHUNKS = 4
SENT = 5
EARLY = 0
WOVEN = 0
Z_ORDER = (4, 3, 5, 2, 6, 1, 7, 0)
XY_ORDER = (4, 3, 5, 2, 6, 1, 7, 0)


def whole_kernel(
    dims,
    q_hbm,
    part_hbm,
    w_hbm,
    rot_hbm,
    dirs_hbm,
    weight_hbm,
    out_hbm,
    nf_hbm,
    rot_ref,
    dirs_row,
    dirs,
    weight,
    ub_ref,
    qext,
    wv,
    send1,
    recv1,
    ext,
    wide,
    pmid,
    send2,
    mid,
    pt,
    rs,
    tt,
    nfb,
    cf,
    ft3,
    wown,
    sem_in,
    sem_hq,
    sem_hqs,
    sem_r1,
    sem_s1,
    sem_rp,
    sem_sp,
    sem_hz,
    sem_hzs,
    sem_hy,
    sem_hys,
    sem_rm,
    sem_sm,
    sem_ro,
    sem_so,
    sem_rt,
    sem_st,
    sem_rn,
    sem_sn,
):
    spaces, groups, nzb, nyb, count, nz, ny, nx = dims
    no = groups * count
    zt, yt = ZT, YT
    per = yt // CHUNKS
    half = yt // 2
    me = lax.axis_index("orient")
    sp = lax.axis_index("space")
    my_zb = me // nyb
    my_yb = me % nyb
    sp_next = lax.rem(sp + 1, spaces)
    sp_prev = lax.rem(sp + spaces - 1, spaces)
    up = my_zb + 1
    z_next = (lax.rem(sp + up // nzb, spaces), lax.rem(up, nzb) * nyb + my_yb)
    down = my_zb + nzb - 1
    z_prev = (
        lax.rem(sp + spaces - 1 + down // nzb, spaces),
        lax.rem(down, nzb) * nyb + my_yb,
    )
    y_next = (sp, my_zb * nyb + lax.rem(my_yb + 1, nyb))
    y_prev = (sp, my_zb * nyb + lax.rem(my_yb + nyb - 1, nyb))

    load_q = pltpu.make_async_copy(q_hbm, qext.at[:, pl.ds(1, nz)], sem_in.at[0])
    load_w = pltpu.make_async_copy(w_hbm, wv, sem_in.at[1])
    loads = [
        pltpu.make_async_copy(dirs_hbm, dirs, sem_in.at[2]),
        pltpu.make_async_copy(dirs_hbm, dirs_row, sem_in.at[3]),
        pltpu.make_async_copy(weight_hbm, weight, sem_in.at[4]),
        pltpu.make_async_copy(rot_hbm, rot_ref, sem_in.at[5]),
    ]
    load_q.start()
    load_w.start()
    for load in loads:
        load.start()

    barrier = pltpu.get_barrier_semaphore()

    def greet(i, carry):
        peer = lax.rem(me + i, groups)
        pl.semaphore_signal(barrier, 1, device_id=(sp, peer), device_id_type=MESH)
        return carry

    for target in (z_next, z_prev, (sp_next, me), (sp_prev, me)):
        pl.semaphore_signal(barrier, 1, device_id=target, device_id_type=MESH)
    lax.fori_loop(1, groups, greet, 0)
    pl.semaphore_wait(barrier, groups + 3)

    def remote(src, dst, ssem, rsem, target):
        return pltpu.make_async_remote_copy(
            src_ref=src,
            dst_ref=dst,
            send_sem=ssem,
            recv_sem=rsem,
            device_id=target,
            device_id_type=MESH,
        )

    remote(
        q_hbm.at[:, pl.ds(nz - 1, 1)], qext.at[:, pl.ds(0, 1)], sem_hqs, sem_hq.at[0], (sp_next, me)
    ).start()
    remote(
        q_hbm.at[:, pl.ds(0, 1)], qext.at[:, pl.ds(nz + 1, 1)], sem_hqs, sem_hq.at[1], (sp_prev, me)
    ).start()

    def part_piece(i, p):
        xy = lax.rem(my_zb + i, nzb)
        slot = lax.rem(nzb - i, nzb)
        return part_hbm.at[:, xy * zt + p], pmid.at[slot, :, p], (sp, xy * nyb + my_yb)

    def ship_part(i, p):
        src, dst, target = part_piece(i, p)
        remote(src, dst, sem_sp, sem_rp, target).start()

    for p in range(zt):
        src, dst, target = part_piece(0, p)
        pltpu.make_async_copy(src, dst, sem_rp).start()

    def ship_parts(first, last):
        def one(n, carry):
            ship_part(1 + n // zt, lax.rem(n, zt))
            return carry

        lax.fori_loop(first, last, one, 0)

    ship_parts(0, EARLY)
    load_q.wait()
    load_w.wait()
    for load in loads:
        load.wait()

    for p in range(zt):

        def advect_plane(i, carry, p=p):
            zb = lax.rem(my_zb + 1 + i, nzb)
            z = zb * zt + p
            if p == 0:

                @pl.when(zb == 0)
                def low_halo():
                    pltpu.make_async_copy(
                        qext.at[:, pl.ds(0, 1)], qext.at[:, pl.ds(0, 1)], sem_hq.at[0]
                    ).wait()

            if p == zt - 1:

                @pl.when(zb == nzb - 1)
                def high_halo():
                    pltpu.make_async_copy(
                        qext.at[:, pl.ds(nz + 1, 1)], qext.at[:, pl.ds(nz + 1, 1)], sem_hq.at[1]
                    ).wait()

            planes = [wv[c, z].astype(F32) for c in range(6)]
            for o in range(count):
                ux = dirs[0, me * count + o]
                uy = dirs[1, me * count + o]
                uz = dirs[2, me * count + o]
                ax = step_length * jnp.maximum(ux, -ux)
                ay = step_length * jnp.maximum(uy, -uy)
                az = step_length * jnp.maximum(uz, -uz)
                terms = (ux * ux, uy * uy, uz * uz, 2.0 * ux * uy, 2.0 * ux * uz, 2.0 * uy * uz)
                f = qext[o, z + 1].astype(F32)
                below = qext[o, z].astype(F32)
                above = qext[o, z + 2].astype(F32)
                up_x = jnp.where(ux > 0.0, pltpu.roll(f, 1, 1), pltpu.roll(f, nx - 1, 1))
                up_y = jnp.where(uy > 0.0, pltpu.roll(f, 1, 0), pltpu.roll(f, ny - 1, 0))
                up_z = jnp.where(uz > 0.0, below, above)
                moved = f * (1.0 - (ax + ay + az)) + ax * up_x + ay * up_y + az * up_z
                power = (-step_length * terms[0]) * planes[0]
                for c in range(1, 6):
                    power = power + (-step_length * terms[c]) * planes[c]
                res = (moved * jnp.exp(power)).astype(BF16)
                for yb in range(nyb):
                    send1[p, zb * nyb + yb, o] = res[yb * yt : (yb + 1) * yt]

            def ship(j, inner):
                yb = lax.rem(my_yb + 1 + j, nyb)
                d = zb * nyb + yb

                @pl.when(d == me)
                def keep():
                    pltpu.make_async_copy(send1.at[p, d], recv1.at[p, me], sem_r1.at[p]).start()

                @pl.when(d != me)
                def send():
                    left = sem_s1.at[i if p == 0 else nzb]
                    remote(send1.at[p, d], recv1.at[p, me], left, sem_r1.at[p], (sp, d)).start()

                return inner

            if p > 0:
                @pl.when(i < nzb - 1)
                def others_left():
                    sent = send1.at[0, pl.ds(0, nyb)]
                    pltpu.make_async_copy(sent, sent, sem_s1.at[i]).wait()

                @pl.when(i == nzb - 1)
                def own_left():
                    sent = send1.at[0, pl.ds(0, nyb - 1)]
                    pltpu.make_async_copy(sent, sent, sem_s1.at[i]).wait()

            lax.fori_loop(0, nyb, ship, 0)
            turn = p * nzb + i - (zt * nzb - WOVEN)

            @pl.when(turn >= 0)
            def weave():
                ship_part(1 + (EARLY + turn) // zt, lax.rem(EARLY + turn, zt))

            return carry

        lax.fori_loop(0, nzb, advect_plane, 0)

    diagonal = lax.broadcasted_iota(jnp.int32, (no, no), 0) == lax.broadcasted_iota(
        jnp.int32, (no, no), 1
    )
    for a in range(3):
        spread = jnp.where(diagonal, jnp.broadcast_to(dirs_row[pl.ds(a, 1), :], (no, no)), 0.0)
        ub_ref[a] = jnp.broadcast_to(jnp.sum(spread, axis=1, keepdims=True), (no, nx))
    ux = ub_ref[0]
    uy = ub_ref[1]
    uz = ub_ref[2]
    ax = step_length * jnp.abs(ux)
    ay = step_length * jnp.abs(uy)
    az = step_length * jnp.abs(uz)
    cf[0] = 1.0 - (ax + ay + az)
    cf[1] = ax
    cf[2] = ay
    cf[3] = az
    lane = lax.broadcasted_iota(jnp.int32, (no, nx), 1)
    terms = (ux * ux, uy * uy, uz * uz, 2.0 * ux * uy, 2.0 * ux * uz, 2.0 * uy * uz)
    packed = jnp.zeros((no, nx), F32)
    for c in range(6):
        value = -step_length * terms[c]
        high = value.astype(BF16).astype(F32)
        rest = value - high
        middle = rest.astype(BF16).astype(F32)
        low = rest - middle
        packed = jnp.where(lane == c, high, packed)
        packed = jnp.where(lane == 8 + c, middle, packed)
        packed = jnp.where(lane == 16 + c, low, packed)
    ft3[...] = packed.astype(BF16)

    wown[...] = jnp.zeros_like(wown)
    for p in range(zt):
        for c in range(6):
            block = wv[c, my_zb * zt + p, pl.ds(pl.multiple_of(my_yb * yt, yt), yt)]
            wown[pl.ds(p * yt * 8 + c, yt, stride=8), :] = block.astype(F32)

    for p in range(zt):
        pltpu.make_async_copy(recv1.at[p], recv1.at[p], sem_r1.at[p]).wait()

        def widen(s, carry, p=p):
            rows = count * yt
            wide[pl.ds(pl.multiple_of(s * rows, rows), rows), :] = (
                recv1[p, s].astype(F32).reshape(rows, nx)
            )
            return carry

        lax.fori_loop(0, groups, widen, 0, unroll=4)
        for chunk in range(CHUNKS):

            def turn(k, carry, p=p, chunk=chunk):
                y = chunk * per + k
                tile = wide[pl.ds(y, no, stride=yt), :].astype(BF16)
                turned = jnp.dot(rot_ref[...], tile, preferred_element_type=F32)
                ext[p + 1, y + 1] = turned.astype(BF16)
                return carry

            lax.fori_loop(0, per, turn, 0, unroll=2)
            rows = pl.ds(1 + chunk * per, per)
            if p == 0:
                remote(
                    ext.at[1, rows], ext.at[zt + 1, rows], sem_hzs, sem_hz.at[1, chunk], z_prev
                ).start()
            if p == zt - 1:
                remote(
                    ext.at[zt, rows], ext.at[0, rows], sem_hzs, sem_hz.at[0, chunk], z_next
                ).start()
            if chunk == 0:
                remote(
                    ext.at[p + 1, pl.ds(1, 1)],
                    ext.at[p + 1, pl.ds(yt + 1, 1)],
                    sem_hys,
                    sem_hy.at[1, p],
                    y_prev,
                ).start()
            if chunk == CHUNKS - 1:
                remote(
                    ext.at[p + 1, pl.ds(yt, 1)],
                    ext.at[p + 1, pl.ds(0, 1)],
                    sem_hys,
                    sem_hy.at[0, p],
                    y_next,
                ).start()

    ship_parts(EARLY + WOVEN, (nzb - 1) * zt)

    def factor(i, carry):
        o = (lax.rem(my_zb + i // count, nzb) * nyb + my_yb) * count + lax.rem(i, count)
        gx = dirs[0, o]
        gy = dirs[1, o]
        gz = dirs[2, o]
        gw = weight[o]
        third = 1.0 / 3.0
        tt[0, i] = (gx * gx - third) * gw
        tt[1, i] = (gy * gy - third) * gw
        tt[2, i] = gx * gy * gw
        tt[3, i] = gx * gz * gw
        tt[4, i] = gy * gz * gw
        return carry

    lax.fori_loop(0, nzb * count, factor, 0)

    def await_copy(ref, sem):
        pltpu.make_async_copy(ref, ref, sem).wait()

    def second_step(p, h):
        face = ext.at[p + 1, pl.ds((yt + 1) * h, 1)]
        await_copy(face, sem_hy.at[h, p])
        for chunk in range(h * CHUNKS // 2, (h + 1) * CHUNKS // 2):
            rows = pl.ds(1 + chunk * per, per)
            if p == zt - 1:
                await_copy(ext.at[zt + 1, rows], sem_hz.at[1, chunk])
            if p == 0:
                await_copy(ext.at[0, rows], sem_hz.at[0, chunk])

            def step(k, carry, chunk=chunk):
                y = chunk * per + k
                f = ext[p + 1, y + 1].astype(F32)
                up_x = jnp.where(ub_ref[0] > 0.0, pltpu.roll(f, 1, 1), pltpu.roll(f, nx - 1, 1))
                up_y = jnp.where(
                    ub_ref[1] > 0.0, ext[p + 1, y].astype(F32), ext[p + 1, y + 2].astype(F32)
                )
                up_z = jnp.where(
                    ub_ref[2] > 0.0, ext[p, y + 1].astype(F32), ext[p + 2, y + 1].astype(F32)
                )
                moved = f * cf[0] + cf[1] * up_x + cf[2] * up_y + cf[3] * up_z
                w8 = wown[pl.ds(pl.multiple_of((p * yt + y) * 8, 8), 8), :]
                w24 = jnp.concatenate([w8, w8, w8], axis=0).astype(BF16)
                power = jnp.dot(ft3[:, :24], w24, preferred_element_type=F32)
                adv = (moved * jnp.exp(power)).astype(BF16)
                turned = jnp.dot(rot_ref[...], adv, preferred_element_type=F32)
                wide[pl.ds(y - h * half, no, stride=half), :] = turned
                return carry

            lax.fori_loop(0, per, step, 0)

        for i in Z_ORDER:
            zc = lax.rem(my_yb + i, nyb)

            def pack(r, carry, zc=zc):
                d = lax.rem(my_zb + r, nzb) * nyb + zc
                rows = count * half
                block = wide[pl.ds(pl.multiple_of(d * rows, rows), rows), :]
                send2[p, h, zc, r] = block.astype(BF16).reshape(count, half, nx)
                return carry

            lax.fori_loop(0, nzb, pack, 0, unroll=4)
            src = send2.at[p, h, zc]
            dst = mid.at[p, h, :, :, my_yb]
            if i == 0:
                pltpu.make_async_copy(src, dst, sem_rm.at[p, h]).start()
            else:
                remote(src, dst, sem_sm, sem_rm.at[p, h], (sp, my_zb * nyb + zc)).start()

    def pass_on(p, h):
        await_copy(mid.at[p, h], sem_rm.at[p, h])
        home = out_hbm.at[:, my_zb * zt + p, :, h]
        for r in XY_ORDER:
            src = mid.at[p, h, r]
            if r == 0:
                pltpu.make_async_copy(src, home, sem_ro).start()
            else:
                xy = lax.rem(my_zb + r, nzb)
                remote(src, home, sem_so, sem_ro, (sp, xy * nyb + my_yb)).start()

    def reduce(p, h):
        for g in range(2):
            blocks = pl.ds(g * nyb // 2, nyb // 2)

            def add_terms(i, sums, blocks=blocks):
                r = i // count
                o = lax.rem(i, count)
                prod = mid[p, h, r, o, blocks].astype(F32) * pmid[r, o, p, blocks, h].astype(F32)
                return tuple(sums[c] + tt[c, i] * prod for c in range(SENT))

            zero = jnp.zeros((nyb // 2, half, nx), F32)
            sums = lax.fori_loop(0, nzb * count, add_terms, (zero,) * SENT)
            for c in range(SENT):
                pt[p, h, blocks, c] = sums[c]
        for i in Z_ORDER:
            zc = lax.rem(my_yb + i, nyb)
            src = pt.at[p, h, zc]
            dst = rs.at[p, h, my_yb]
            if i == 0:
                pltpu.make_async_copy(src, dst, sem_rt.at[p, h]).start()
            else:
                remote(src, dst, sem_st, sem_rt.at[p, h], (sp, my_zb * nyb + zc)).start()

    nf_home = nf_hbm.at[:, pl.ds(my_zb * zt, zt)]
    each = nyb // 2

    def relax(p, h):
        await_copy(rs.at[p, h], sem_rt.at[p, h])
        totals = []
        for c in range(SENT):
            total = rs[p, h, 0, c]
            for s in range(1, nyb):
                total = total + rs[p, h, s, c]
            totals.append(total)
        totals.insert(2, -(totals[0] + totals[1]))
        for c in range(6):
            total = totals[c]
            old = wv[c, my_zb * zt + p, pl.ds(pl.multiple_of(my_yb * yt, yt), yt)].astype(F32)
            old = old[h * half : (h + 1) * half]
            value = (1.0 - relax_rate) * old + relax_rate * coupling * total
            for j in range(each):
                nfb[h * each + j, c, p] = value[2 * j : 2 * j + 2]
        if p == 0:

            def ship_field(j, carry):
                k = my_yb * nyb + j

                @pl.when(k == me)
                def keep():
                    pltpu.make_async_copy(nfb.at[j], nf_home, sem_rn).start()

                @pl.when(k != me)
                def send():
                    remote(nfb.at[j], nf_home, sem_sn, sem_rn, (sp, k)).start()

                return carry

            lax.fori_loop(h * each, (h + 1) * each, ship_field, 0)

    second_step(1, 0)
    second_step(1, 1)
    second_step(0, 0)
    pass_on(1, 0)
    second_step(0, 1)
    pass_on(1, 1)
    await_copy(pmid, sem_rp)
    reduce(1, 0)
    reduce(1, 1)
    pass_on(0, 0)
    reduce(0, 0)
    relax(1, 0)
    relax(1, 1)
    pass_on(0, 1)
    reduce(0, 1)
    relax(0, 0)
    relax(0, 1)

    def drain(ref, sem):
        pltpu.make_async_copy(ref, ref, sem).wait()

    drain(nf_hbm, sem_rn)
    drain(out_hbm, sem_ro)
    drain(qext.at[:, pl.ds(0, 2)], sem_hqs)
    drain(send1.at[1, pl.ds(0, groups - 1)], sem_s1.at[nzb])
    drain(pmid.at[pl.ds(0, nzb - 1)], sem_sp)
    drain(ext.at[pl.ds(0, 2), pl.ds(1, yt)], sem_hzs)
    drain(ext.at[0, pl.ds(0, 4)], sem_hys)
    drain(send2.at[:, :, pl.ds(0, nyb - 1)], sem_sm)
    drain(mid.at[:, :, pl.ds(0, nzb - 1)], sem_so)
    drain(pt.at[:, :, pl.ds(0, nyb - 1)], sem_st)

    sent_self = my_zb == my_yb

    @pl.when(sent_self)
    def drain_most():
        drain(nfb.at[pl.ds(0, nyb - 1)], sem_sn)

    @pl.when(jnp.logical_not(sent_self))
    def drain_all():
        drain(nfb, sem_sn)


def per_device(q_init, partner, field, orientations, orient_weight, rotation):
    count, nz, ny, nx = q_init.shape
    no = orientations.shape[1]
    nzb, nyb = nz // ZT, ny // YT
    groups = lax.axis_size("orient")
    spaces = lax.axis_size("space")
    dims = (spaces, groups, nzb, nyb, count, nz, ny, nx)
    pairs = ny // groups
    hbm = pl.BlockSpec(memory_space=pltpu.HBM)
    anywhere = pl.BlockSpec(memory_space=pltpu.VMEM)
    dma = pltpu.SemaphoreType.DMA
    part = partner.reshape(count, nz, nyb, 2, YT // 2, nx)
    out, new_field = pl.pallas_call(
        functools.partial(whole_kernel, dims),
        in_specs=[hbm] * 6,
        out_specs=[anywhere, anywhere],
        out_shape=[
            jax.ShapeDtypeStruct((count, nz, nyb, 2, YT // 2, nx), BF16),
            jax.ShapeDtypeStruct((6, nz, pairs, nx), F32),
        ],
        scratch_shapes=[
            pltpu.VMEM((no, no), BF16),
            pltpu.VMEM((3, no), F32),
            pltpu.SMEM((3, no), F32),
            pltpu.SMEM((no,), F32),
            pltpu.VMEM((3, no, nx), F32),
            pltpu.VMEM((count, nz + 2, ny, nx), BF16),
            pltpu.VMEM((6, nz, ny, nx), BF16),
            pltpu.VMEM((ZT, groups, count, YT, nx), BF16),
            pltpu.VMEM((ZT, groups, count, YT, nx), BF16),
            pltpu.VMEM((ZT + 2, YT + 2, no, nx), BF16),
            pltpu.VMEM((no * YT, nx), F32),
            pltpu.VMEM((nzb, count, ZT, nyb, 2, YT // 2, nx), BF16),
            pltpu.VMEM((ZT, 2, nyb, nzb, count, YT // 2, nx), BF16),
            pltpu.VMEM((ZT, 2, nzb, count, nyb, YT // 2, nx), BF16),
            pltpu.VMEM((ZT, 2, nyb, SENT, YT // 2, nx), F32),
            pltpu.VMEM((ZT, 2, nyb, SENT, YT // 2, nx), F32),
            pltpu.SMEM((SENT, nzb * count), F32),
            pltpu.VMEM((nyb, 6, ZT, pairs, nx), F32),
            pltpu.VMEM((4, no, nx), F32),
            pltpu.VMEM((no, nx), BF16),
            pltpu.VMEM((ZT * YT * 8, nx), F32),
            dma((6,)),
            dma((2,)),
            dma(()),
            dma((ZT,)),
            dma((nzb + 1,)),
            dma(()),
            dma(()),
            dma((2, CHUNKS)),
            dma(()),
            dma((2, ZT)),
            dma(()),
            dma((ZT, 2)),
            dma(()),
            dma(()),
            dma(()),
            dma((ZT, 2)),
            dma(()),
            dma(()),
            dma(()),
        ],
        compiler_params=pltpu.CompilerParams(
            collective_id=0, has_side_effects=True, vmem_limit_bytes=40 << 20
        ),
        name="whole",
    )(
        *[
            pltpu.with_memory_space_constraint(x, pltpu.HBM)
            for x in (q_init, part, field, rotation, orientations, orient_weight)
        ]
    )
    return out.reshape(count, nz, ny, nx), new_field


def solution(mesh):
    in_specs = (
        P("orient", "space", None, None),
        P("orient", "space", None, None),
        P(None, "space", None, None),
        P(),
        P(),
        P(),
    )
    out_specs = (P("orient", "space", None, None), P(None, "space", "orient", None))
    return jax.shard_map(
        per_device, mesh=mesh, in_specs=in_specs, out_specs=out_specs, check_vma=False
    )
```

```python
import functools

import jax
import jax.numpy as jnp
from jax import lax
from jax.experimental import pallas as pl
from jax.experimental.pallas import tpu as pltpu
from jax.sharding import PartitionSpec as P

step_length = 0.3
relax_rate = 0.5
coupling = 8.0

F32 = jnp.float32
BF16 = jnp.bfloat16
MESH = pl.DeviceIdType.MESH
ZT = 2
YT = 16
CHUNKS = 4
SENT = 5
EARLY = 0
WOVEN = 0
Z_ORDER = (4, 3, 5, 2, 6, 1, 7, 0)
XY_ORDER = (0, 1, 7, 2, 6, 3, 5, 4)


def whole_kernel(
    dims,
    q_hbm,
    part_hbm,
    w_hbm,
    rot_hbm,
    dirs_hbm,
    weight_hbm,
    out_hbm,
    nf_hbm,
    rot_ref,
    dirs_row,
    dirs,
    weight,
    ub_ref,
    qext,
    wv,
    send1,
    recv1,
    ext,
    wide,
    pmid,
    send2,
    mid,
    pt,
    rs,
    tt,
    nfb,
    cf,
    ft3,
    wown,
    sem_in,
    sem_hq,
    sem_hqs,
    sem_r1,
    sem_s1,
    sem_rp,
    sem_sp,
    sem_hz,
    sem_hzs,
    sem_hy,
    sem_hys,
    sem_rm,
    sem_sm,
    sem_ro,
    sem_so,
    sem_rt,
    sem_st,
    sem_rn,
    sem_sn,
):
    spaces, groups, nzb, nyb, count, nz, ny, nx = dims
    no = groups * count
    zt, yt = ZT, YT
    per = yt // CHUNKS
    half = yt // 2
    me = lax.axis_index("orient")
    sp = lax.axis_index("space")
    my_zb = me // nyb
    my_yb = me % nyb
    sp_next = lax.rem(sp + 1, spaces)
    sp_prev = lax.rem(sp + spaces - 1, spaces)
    up = my_zb + 1
    z_next = (lax.rem(sp + up // nzb, spaces), lax.rem(up, nzb) * nyb + my_yb)
    down = my_zb + nzb - 1
    z_prev = (
        lax.rem(sp + spaces - 1 + down // nzb, spaces),
        lax.rem(down, nzb) * nyb + my_yb,
    )
    y_next = (sp, my_zb * nyb + lax.rem(my_yb + 1, nyb))
    y_prev = (sp, my_zb * nyb + lax.rem(my_yb + nyb - 1, nyb))

    load_q = pltpu.make_async_copy(q_hbm, qext.at[:, pl.ds(1, nz)], sem_in.at[0])
    load_w = pltpu.make_async_copy(w_hbm, wv, sem_in.at[1])
    loads = [
        pltpu.make_async_copy(dirs_hbm, dirs, sem_in.at[2]),
        pltpu.make_async_copy(dirs_hbm, dirs_row, sem_in.at[3]),
        pltpu.make_async_copy(weight_hbm, weight, sem_in.at[4]),
        pltpu.make_async_copy(rot_hbm, rot_ref, sem_in.at[5]),
    ]
    load_q.start()
    load_w.start()
    for load in loads:
        load.start()

    barrier = pltpu.get_barrier_semaphore()

    def greet(i, carry):
        peer = lax.rem(me + i, groups)
        pl.semaphore_signal(barrier, 1, device_id=(sp, peer), device_id_type=MESH)
        return carry

    for target in (z_next, z_prev, (sp_next, me), (sp_prev, me)):
        pl.semaphore_signal(barrier, 1, device_id=target, device_id_type=MESH)
    lax.fori_loop(1, groups, greet, 0)
    pl.semaphore_wait(barrier, groups + 3)

    def remote(src, dst, ssem, rsem, target):
        return pltpu.make_async_remote_copy(
            src_ref=src,
            dst_ref=dst,
            send_sem=ssem,
            recv_sem=rsem,
            device_id=target,
            device_id_type=MESH,
        )

    remote(
        q_hbm.at[:, pl.ds(nz - 1, 1)], qext.at[:, pl.ds(0, 1)], sem_hqs, sem_hq.at[0], (sp_next, me)
    ).start()
    remote(
        q_hbm.at[:, pl.ds(0, 1)], qext.at[:, pl.ds(nz + 1, 1)], sem_hqs, sem_hq.at[1], (sp_prev, me)
    ).start()

    def part_piece(i, p):
        xy = lax.rem(my_zb + i, nzb)
        slot = lax.rem(nzb - i, nzb)
        return part_hbm.at[:, xy * zt + p], pmid.at[slot, :, p], (sp, xy * nyb + my_yb)

    def ship_part(i, p):
        src, dst, target = part_piece(i, p)
        remote(src, dst, sem_sp, sem_rp, target).start()

    for p in range(zt):
        src, dst, target = part_piece(0, p)
        pltpu.make_async_copy(src, dst, sem_rp).start()

    def ship_parts(first, last):
        def one(n, carry):
            ship_part(1 + n // zt, lax.rem(n, zt))
            return carry

        lax.fori_loop(first, last, one, 0)

    ship_parts(0, EARLY)
    load_q.wait()
    load_w.wait()
    for load in loads:
        load.wait()

    for p in range(zt):

        def advect_plane(i, carry, p=p):
            zb = lax.rem(my_zb + 1 + i, nzb)
            z = zb * zt + p
            if p == 0:

                @pl.when(zb == 0)
                def low_halo():
                    pltpu.make_async_copy(
                        qext.at[:, pl.ds(0, 1)], qext.at[:, pl.ds(0, 1)], sem_hq.at[0]
                    ).wait()

            if p == zt - 1:

                @pl.when(zb == nzb - 1)
                def high_halo():
                    pltpu.make_async_copy(
                        qext.at[:, pl.ds(nz + 1, 1)], qext.at[:, pl.ds(nz + 1, 1)], sem_hq.at[1]
                    ).wait()

            planes = [wv[c, z].astype(F32) for c in range(6)]
            for o in range(count):
                ux = dirs[0, me * count + o]
                uy = dirs[1, me * count + o]
                uz = dirs[2, me * count + o]
                ax = step_length * jnp.maximum(ux, -ux)
                ay = step_length * jnp.maximum(uy, -uy)
                az = step_length * jnp.maximum(uz, -uz)
                terms = (ux * ux, uy * uy, uz * uz, 2.0 * ux * uy, 2.0 * ux * uz, 2.0 * uy * uz)
                f = qext[o, z + 1].astype(F32)
                below = qext[o, z].astype(F32)
                above = qext[o, z + 2].astype(F32)
                up_x = jnp.where(ux > 0.0, pltpu.roll(f, 1, 1), pltpu.roll(f, nx - 1, 1))
                up_y = jnp.where(uy > 0.0, pltpu.roll(f, 1, 0), pltpu.roll(f, ny - 1, 0))
                up_z = jnp.where(uz > 0.0, below, above)
                moved = f * (1.0 - (ax + ay + az)) + ax * up_x + ay * up_y + az * up_z
                power = (-step_length * terms[0]) * planes[0]
                for c in range(1, 6):
                    power = power + (-step_length * terms[c]) * planes[c]
                res = (moved * jnp.exp(power)).astype(BF16)
                for yb in range(nyb):
                    send1[p, zb * nyb + yb, o] = res[yb * yt : (yb + 1) * yt]

            def ship(j, inner):
                yb = lax.rem(my_yb + 1 + j, nyb)
                d = zb * nyb + yb

                @pl.when(d == me)
                def keep():
                    pltpu.make_async_copy(send1.at[p, d], recv1.at[p, me], sem_r1.at[p]).start()

                @pl.when(d != me)
                def send():
                    left = sem_s1.at[i if p == 0 else nzb]
                    remote(send1.at[p, d], recv1.at[p, me], left, sem_r1.at[p], (sp, d)).start()

                return inner

            if p > 0:
                @pl.when(i < nzb - 1)
                def others_left():
                    sent = send1.at[0, pl.ds(0, nyb)]
                    pltpu.make_async_copy(sent, sent, sem_s1.at[i]).wait()

                @pl.when(i == nzb - 1)
                def own_left():
                    sent = send1.at[0, pl.ds(0, nyb - 1)]
                    pltpu.make_async_copy(sent, sent, sem_s1.at[i]).wait()

            lax.fori_loop(0, nyb, ship, 0)
            turn = p * nzb + i - (zt * nzb - WOVEN)

            @pl.when(turn >= 0)
            def weave():
                ship_part(1 + (EARLY + turn) // zt, lax.rem(EARLY + turn, zt))

            return carry

        lax.fori_loop(0, nzb, advect_plane, 0)

    diagonal = lax.broadcasted_iota(jnp.int32, (no, no), 0) == lax.broadcasted_iota(
        jnp.int32, (no, no), 1
    )
    for a in range(3):
        spread = jnp.where(diagonal, jnp.broadcast_to(dirs_row[pl.ds(a, 1), :], (no, no)), 0.0)
        ub_ref[a] = jnp.broadcast_to(jnp.sum(spread, axis=1, keepdims=True), (no, nx))
    ux = ub_ref[0]
    uy = ub_ref[1]
    uz = ub_ref[2]
    ax = step_length * jnp.abs(ux)
    ay = step_length * jnp.abs(uy)
    az = step_length * jnp.abs(uz)
    cf[0] = 1.0 - (ax + ay + az)
    cf[1] = ax
    cf[2] = ay
    cf[3] = az
    lane = lax.broadcasted_iota(jnp.int32, (no, nx), 1)
    terms = (ux * ux, uy * uy, uz * uz, 2.0 * ux * uy, 2.0 * ux * uz, 2.0 * uy * uz)
    packed = jnp.zeros((no, nx), F32)
    for c in range(6):
        value = -step_length * terms[c]
        high = value.astype(BF16).astype(F32)
        rest = value - high
        middle = rest.astype(BF16).astype(F32)
        low = rest - middle
        packed = jnp.where(lane == c, high, packed)
        packed = jnp.where(lane == 8 + c, middle, packed)
        packed = jnp.where(lane == 16 + c, low, packed)
    ft3[...] = packed.astype(BF16)

    wown[...] = jnp.zeros_like(wown)
    for p in range(zt):
        for c in range(6):
            block = wv[c, my_zb * zt + p, pl.ds(pl.multiple_of(my_yb * yt, yt), yt)]
            wown[pl.ds(p * yt * 8 + c, yt, stride=8), :] = block.astype(F32)

    for p in range(zt):
        pltpu.make_async_copy(recv1.at[p], recv1.at[p], sem_r1.at[p]).wait()

        def widen(s, carry, p=p):
            rows = count * yt
            wide[pl.ds(pl.multiple_of(s * rows, rows), rows), :] = (
                recv1[p, s].astype(F32).reshape(rows, nx)
            )
            return carry

        lax.fori_loop(0, groups, widen, 0, unroll=4)
        for chunk in range(CHUNKS):

            def turn(k, carry, p=p, chunk=chunk):
                y = chunk * per + k
                tile = wide[pl.ds(y, no, stride=yt), :].astype(BF16)
                turned = jnp.dot(rot_ref[...], tile, preferred_element_type=F32)
                ext[p + 1, y + 1] = turned.astype(BF16)
                return carry

            lax.fori_loop(0, per, turn, 0, unroll=2)
            rows = pl.ds(1 + chunk * per, per)
            if p == 0:
                remote(
                    ext.at[1, rows], ext.at[zt + 1, rows], sem_hzs, sem_hz.at[1, chunk], z_prev
                ).start()
            if p == zt - 1:
                remote(
                    ext.at[zt, rows], ext.at[0, rows], sem_hzs, sem_hz.at[0, chunk], z_next
                ).start()
            if chunk == 0:
                remote(
                    ext.at[p + 1, pl.ds(1, 1)],
                    ext.at[p + 1, pl.ds(yt + 1, 1)],
                    sem_hys,
                    sem_hy.at[1, p],
                    y_prev,
                ).start()
            if chunk == CHUNKS - 1:
                remote(
                    ext.at[p + 1, pl.ds(yt, 1)],
                    ext.at[p + 1, pl.ds(0, 1)],
                    sem_hys,
                    sem_hy.at[0, p],
                    y_next,
                ).start()

    ship_parts(EARLY + WOVEN, (nzb - 1) * zt)

    def factor(i, carry):
        o = (lax.rem(my_zb + i // count, nzb) * nyb + my_yb) * count + lax.rem(i, count)
        gx = dirs[0, o]
        gy = dirs[1, o]
        gz = dirs[2, o]
        gw = weight[o]
        third = 1.0 / 3.0
        tt[0, i] = (gx * gx - third) * gw
        tt[1, i] = (gy * gy - third) * gw
        tt[2, i] = gx * gy * gw
        tt[3, i] = gx * gz * gw
        tt[4, i] = gy * gz * gw
        return carry

    lax.fori_loop(0, nzb * count, factor, 0)

    def await_copy(ref, sem):
        pltpu.make_async_copy(ref, ref, sem).wait()

    def second_step(p, h):
        face = ext.at[p + 1, pl.ds((yt + 1) * h, 1)]
        await_copy(face, sem_hy.at[h, p])
        for chunk in range(h * CHUNKS // 2, (h + 1) * CHUNKS // 2):
            rows = pl.ds(1 + chunk * per, per)
            if p == zt - 1:
                await_copy(ext.at[zt + 1, rows], sem_hz.at[1, chunk])
            if p == 0:
                await_copy(ext.at[0, rows], sem_hz.at[0, chunk])

            def step(k, carry, chunk=chunk):
                y = chunk * per + k
                f = ext[p + 1, y + 1].astype(F32)
                up_x = jnp.where(ub_ref[0] > 0.0, pltpu.roll(f, 1, 1), pltpu.roll(f, nx - 1, 1))
                up_y = jnp.where(
                    ub_ref[1] > 0.0, ext[p + 1, y].astype(F32), ext[p + 1, y + 2].astype(F32)
                )
                up_z = jnp.where(
                    ub_ref[2] > 0.0, ext[p, y + 1].astype(F32), ext[p + 2, y + 1].astype(F32)
                )
                moved = f * cf[0] + cf[1] * up_x + cf[2] * up_y + cf[3] * up_z
                w8 = wown[pl.ds(pl.multiple_of((p * yt + y) * 8, 8), 8), :]
                w24 = jnp.concatenate([w8, w8, w8], axis=0).astype(BF16)
                power = jnp.dot(ft3[:, :24], w24, preferred_element_type=F32)
                adv = (moved * jnp.exp(power)).astype(BF16)
                turned = jnp.dot(rot_ref[...], adv, preferred_element_type=F32)
                wide[pl.ds(y - h * half, no, stride=half), :] = turned
                return carry

            lax.fori_loop(0, per, step, 0)

        for i in Z_ORDER:
            zc = lax.rem(my_yb + i, nyb)

            def pack(r, carry, zc=zc):
                d = lax.rem(my_zb + r, nzb) * nyb + zc
                rows = count * half
                block = wide[pl.ds(pl.multiple_of(d * rows, rows), rows), :]
                send2[p, h, zc, r] = block.astype(BF16).reshape(count, half, nx)
                return carry

            lax.fori_loop(0, nzb, pack, 0, unroll=4)
            src = send2.at[p, h, zc]
            dst = mid.at[p, h, :, :, my_yb]
            if i == 0:
                pltpu.make_async_copy(src, dst, sem_rm.at[p, h]).start()
            else:
                remote(src, dst, sem_sm, sem_rm.at[p, h], (sp, my_zb * nyb + zc)).start()

    def pass_on(p, h):
        await_copy(mid.at[p, h], sem_rm.at[p, h])
        home = out_hbm.at[:, my_zb * zt + p, :, h]
        for r in XY_ORDER:
            src = mid.at[p, h, r]
            if r == 0:
                pltpu.make_async_copy(src, home, sem_ro).start()
            else:
                xy = lax.rem(my_zb + r, nzb)
                remote(src, home, sem_so, sem_ro, (sp, xy * nyb + my_yb)).start()

    def reduce(p, h):
        for g in range(2):
            blocks = pl.ds(g * nyb // 2, nyb // 2)

            def add_terms(r, sums, blocks=blocks):
                for o in range(count):
                    prod = mid[p, h, r, o, blocks].astype(F32)
                    prod = prod * pmid[r, o, p, blocks, h].astype(F32)
                    sums = [sums[c] + tt[c, r * count + o] * prod for c in range(SENT)]
                return tuple(sums)

            zero = jnp.zeros((nyb // 2, half, nx), F32)
            sums = lax.fori_loop(0, nzb, add_terms, (zero,) * SENT, unroll=1)
            for c in range(SENT):
                pt[p, h, blocks, c] = sums[c]
        for i in Z_ORDER:
            zc = lax.rem(my_yb + i, nyb)
            src = pt.at[p, h, zc]
            dst = rs.at[p, h, my_yb]
            if i == 0:
                pltpu.make_async_copy(src, dst, sem_rt.at[p, h]).start()
            else:
                remote(src, dst, sem_st, sem_rt.at[p, h], (sp, my_zb * nyb + zc)).start()

    nf_home = nf_hbm.at[:, pl.ds(my_zb * zt, zt)]
    each = nyb // 2

    def relax(p, h):
        await_copy(rs.at[p, h], sem_rt.at[p, h])
        totals = []
        for c in range(SENT):
            total = rs[p, h, 0, c]
            for s in range(1, nyb):
                total = total + rs[p, h, s, c]
            totals.append(total)
        totals.insert(2, -(totals[0] + totals[1]))
        for c in range(6):
            total = totals[c]
            old = wv[c, my_zb * zt + p, pl.ds(pl.multiple_of(my_yb * yt, yt), yt)].astype(F32)
            old = old[h * half : (h + 1) * half]
            value = (1.0 - relax_rate) * old + relax_rate * coupling * total
            for j in range(each):
                nfb[h * each + j, c, p] = value[2 * j : 2 * j + 2]
        if p == 0:

            def ship_field(j, carry):
                k = my_yb * nyb + j

                @pl.when(k == me)
                def keep():
                    pltpu.make_async_copy(nfb.at[j], nf_home, sem_rn).start()

                @pl.when(k != me)
                def send():
                    remote(nfb.at[j], nf_home, sem_sn, sem_rn, (sp, k)).start()

                return carry

            lax.fori_loop(h * each, (h + 1) * each, ship_field, 0)

    second_step(1, 0)
    second_step(1, 1)
    second_step(0, 0)
    second_step(0, 1)
    pass_on(1, 0)
    await_copy(pmid, sem_rp)
    reduce(1, 0)
    pass_on(1, 1)
    reduce(1, 1)
    pass_on(0, 0)
    reduce(0, 0)
    pass_on(0, 1)
    reduce(0, 1)
    relax(1, 0)
    relax(1, 1)
    relax(0, 0)
    relax(0, 1)

    def drain(ref, sem):
        pltpu.make_async_copy(ref, ref, sem).wait()

    drain(nf_hbm, sem_rn)
    drain(out_hbm, sem_ro)
    drain(qext.at[:, pl.ds(0, 2)], sem_hqs)
    drain(send1.at[1, pl.ds(0, groups - 1)], sem_s1.at[nzb])
    drain(pmid.at[pl.ds(0, nzb - 1)], sem_sp)
    drain(ext.at[pl.ds(0, 2), pl.ds(1, yt)], sem_hzs)
    drain(ext.at[0, pl.ds(0, 4)], sem_hys)
    drain(send2.at[:, :, pl.ds(0, nyb - 1)], sem_sm)
    drain(mid.at[:, :, pl.ds(0, nzb - 1)], sem_so)
    drain(pt.at[:, :, pl.ds(0, nyb - 1)], sem_st)

    sent_self = my_zb == my_yb

    @pl.when(sent_self)
    def drain_most():
        drain(nfb.at[pl.ds(0, nyb - 1)], sem_sn)

    @pl.when(jnp.logical_not(sent_self))
    def drain_all():
        drain(nfb, sem_sn)


def per_device(q_init, partner, field, orientations, orient_weight, rotation):
    count, nz, ny, nx = q_init.shape
    no = orientations.shape[1]
    nzb, nyb = nz // ZT, ny // YT
    groups = lax.axis_size("orient")
    spaces = lax.axis_size("space")
    dims = (spaces, groups, nzb, nyb, count, nz, ny, nx)
    pairs = ny // groups
    hbm = pl.BlockSpec(memory_space=pltpu.HBM)
    anywhere = pl.BlockSpec(memory_space=pltpu.VMEM)
    dma = pltpu.SemaphoreType.DMA
    part = partner.reshape(count, nz, nyb, 2, YT // 2, nx)
    out, new_field = pl.pallas_call(
        functools.partial(whole_kernel, dims),
        in_specs=[hbm] * 6,
        out_specs=[anywhere, anywhere],
        out_shape=[
            jax.ShapeDtypeStruct((count, nz, nyb, 2, YT // 2, nx), BF16),
            jax.ShapeDtypeStruct((6, nz, pairs, nx), F32),
        ],
        scratch_shapes=[
            pltpu.VMEM((no, no), BF16),
            pltpu.VMEM((3, no), F32),
            pltpu.SMEM((3, no), F32),
            pltpu.SMEM((no,), F32),
            pltpu.VMEM((3, no, nx), F32),
            pltpu.VMEM((count, nz + 2, ny, nx), BF16),
            pltpu.VMEM((6, nz, ny, nx), BF16),
            pltpu.VMEM((ZT, groups, count, YT, nx), BF16),
            pltpu.VMEM((ZT, groups, count, YT, nx), BF16),
            pltpu.VMEM((ZT + 2, YT + 2, no, nx), BF16),
            pltpu.VMEM((no * YT, nx), F32),
            pltpu.VMEM((nzb, count, ZT, nyb, 2, YT // 2, nx), BF16),
            pltpu.VMEM((ZT, 2, nyb, nzb, count, YT // 2, nx), BF16),
            pltpu.VMEM((ZT, 2, nzb, count, nyb, YT // 2, nx), BF16),
            pltpu.VMEM((ZT, 2, nyb, SENT, YT // 2, nx), F32),
            pltpu.VMEM((ZT, 2, nyb, SENT, YT // 2, nx), F32),
            pltpu.SMEM((SENT, nzb * count), F32),
            pltpu.VMEM((nyb, 6, ZT, pairs, nx), F32),
            pltpu.VMEM((4, no, nx), F32),
            pltpu.VMEM((no, nx), BF16),
            pltpu.VMEM((ZT * YT * 8, nx), F32),
            dma((6,)),
            dma((2,)),
            dma(()),
            dma((ZT,)),
            dma((nzb + 1,)),
            dma(()),
            dma(()),
            dma((2, CHUNKS)),
            dma(()),
            dma((2, ZT)),
            dma(()),
            dma((ZT, 2)),
            dma(()),
            dma(()),
            dma(()),
            dma((ZT, 2)),
            dma(()),
            dma(()),
            dma(()),
        ],
        compiler_params=pltpu.CompilerParams(
            collective_id=0, has_side_effects=True, vmem_limit_bytes=40 << 20
        ),
        name="whole",
    )(
        *[
            pltpu.with_memory_space_constraint(x, pltpu.HBM)
            for x in (q_init, part, field, rotation, orientations, orient_weight)
        ]
    )
    return out.reshape(count, nz, ny, nx), new_field


def solution(mesh):
    in_specs = (
        P("orient", "space", None, None),
        P("orient", "space", None, None),
        P(None, "space", None, None),
        P(),
        P(),
        P(),
    )
    out_specs = (P("orient", "space", None, None), P(None, "space", "orient", None))
    return jax.shard_map(
        per_device, mesh=mesh, in_specs=in_specs, out_specs=out_specs, check_vma=False
    )
```

```python
import functools

import jax
import jax.numpy as jnp
from jax import lax
from jax.experimental import pallas as pl
from jax.experimental.pallas import tpu as pltpu
from jax.sharding import PartitionSpec as P

step_length = 0.3
relax_rate = 0.5
coupling = 8.0

F32 = jnp.float32
BF16 = jnp.bfloat16
MESH = pl.DeviceIdType.MESH
ZT = 2
YT = 16
CHUNKS = 4
SENT = 5
EARLY = 0
WOVEN = 0
SOON = 6
Z_ORDER = (4, 3, 5, 2, 6, 1, 7, 0)
XY_ORDER = (0, 1, 7, 2, 6, 3, 5, 4)


def whole_kernel(
    dims,
    q_hbm,
    part_hbm,
    w_hbm,
    rot_hbm,
    dirs_hbm,
    weight_hbm,
    out_hbm,
    nf_hbm,
    rot_ref,
    dirs_row,
    dirs,
    weight,
    ub_ref,
    qext,
    wv,
    send1,
    recv1,
    ext,
    wide,
    pmid,
    send2,
    mid,
    pt,
    rs,
    tt,
    nfb,
    cf,
    ft3,
    wown,
    sem_in,
    sem_hq,
    sem_hqs,
    sem_r1,
    sem_s1,
    sem_rp,
    sem_sp,
    sem_hz,
    sem_hzs,
    sem_hy,
    sem_hys,
    sem_rm,
    sem_sm,
    sem_ro,
    sem_so,
    sem_rt,
    sem_st,
    sem_rn,
    sem_sn,
):
    spaces, groups, nzb, nyb, count, nz, ny, nx = dims
    no = groups * count
    zt, yt = ZT, YT
    per = yt // CHUNKS
    half = yt // 2
    me = lax.axis_index("orient")
    sp = lax.axis_index("space")
    my_zb = me // nyb
    my_yb = me % nyb
    sp_next = lax.rem(sp + 1, spaces)
    sp_prev = lax.rem(sp + spaces - 1, spaces)
    up = my_zb + 1
    z_next = (lax.rem(sp + up // nzb, spaces), lax.rem(up, nzb) * nyb + my_yb)
    down = my_zb + nzb - 1
    z_prev = (
        lax.rem(sp + spaces - 1 + down // nzb, spaces),
        lax.rem(down, nzb) * nyb + my_yb,
    )
    y_next = (sp, my_zb * nyb + lax.rem(my_yb + 1, nyb))
    y_prev = (sp, my_zb * nyb + lax.rem(my_yb + nyb - 1, nyb))

    load_q = pltpu.make_async_copy(q_hbm, qext.at[:, pl.ds(1, nz)], sem_in.at[0])
    load_w = pltpu.make_async_copy(w_hbm, wv, sem_in.at[1])
    loads = [
        pltpu.make_async_copy(dirs_hbm, dirs, sem_in.at[2]),
        pltpu.make_async_copy(dirs_hbm, dirs_row, sem_in.at[3]),
        pltpu.make_async_copy(weight_hbm, weight, sem_in.at[4]),
        pltpu.make_async_copy(rot_hbm, rot_ref, sem_in.at[5]),
    ]
    load_q.start()
    load_w.start()
    for load in loads:
        load.start()

    barrier = pltpu.get_barrier_semaphore()

    def greet(i, carry):
        peer = lax.rem(me + i, groups)
        pl.semaphore_signal(barrier, 1, device_id=(sp, peer), device_id_type=MESH)
        return carry

    for target in (z_next, z_prev, (sp_next, me), (sp_prev, me)):
        pl.semaphore_signal(barrier, 1, device_id=target, device_id_type=MESH)
    lax.fori_loop(1, groups, greet, 0)
    pl.semaphore_wait(barrier, groups + 3)

    def remote(src, dst, ssem, rsem, target):
        return pltpu.make_async_remote_copy(
            src_ref=src,
            dst_ref=dst,
            send_sem=ssem,
            recv_sem=rsem,
            device_id=target,
            device_id_type=MESH,
        )

    remote(
        q_hbm.at[:, pl.ds(nz - 1, 1)], qext.at[:, pl.ds(0, 1)], sem_hqs, sem_hq.at[0], (sp_next, me)
    ).start()
    remote(
        q_hbm.at[:, pl.ds(0, 1)], qext.at[:, pl.ds(nz + 1, 1)], sem_hqs, sem_hq.at[1], (sp_prev, me)
    ).start()

    def part_piece(i, p):
        xy = lax.rem(my_zb + i, nzb)
        slot = lax.rem(nzb - i, nzb)
        return part_hbm.at[:, xy * zt + p], pmid.at[slot, :, p], (sp, xy * nyb + my_yb)

    def ship_part(i, p):
        src, dst, target = part_piece(i, p)
        remote(src, dst, sem_sp, sem_rp, target).start()

    for p in range(zt):
        src, dst, target = part_piece(0, p)
        pltpu.make_async_copy(src, dst, sem_rp).start()

    def ship_parts(first, last):
        def one(n, carry):
            ship_part(1 + n // zt, lax.rem(n, zt))
            return carry

        lax.fori_loop(first, last, one, 0)

    ship_parts(0, EARLY)
    load_q.wait()
    load_w.wait()
    for load in loads:
        load.wait()

    for p in range(zt):

        def advect_plane(i, carry, p=p):
            zb = lax.rem(my_zb + 1 + i, nzb)
            z = zb * zt + p
            if p == 0:

                @pl.when(zb == 0)
                def low_halo():
                    pltpu.make_async_copy(
                        qext.at[:, pl.ds(0, 1)], qext.at[:, pl.ds(0, 1)], sem_hq.at[0]
                    ).wait()

            if p == zt - 1:

                @pl.when(zb == nzb - 1)
                def high_halo():
                    pltpu.make_async_copy(
                        qext.at[:, pl.ds(nz + 1, 1)], qext.at[:, pl.ds(nz + 1, 1)], sem_hq.at[1]
                    ).wait()

            planes = [wv[c, z].astype(F32) for c in range(6)]
            for o in range(count):
                ux = dirs[0, me * count + o]
                uy = dirs[1, me * count + o]
                uz = dirs[2, me * count + o]
                ax = step_length * jnp.maximum(ux, -ux)
                ay = step_length * jnp.maximum(uy, -uy)
                az = step_length * jnp.maximum(uz, -uz)
                terms = (ux * ux, uy * uy, uz * uz, 2.0 * ux * uy, 2.0 * ux * uz, 2.0 * uy * uz)
                f = qext[o, z + 1].astype(F32)
                below = qext[o, z].astype(F32)
                above = qext[o, z + 2].astype(F32)
                up_x = jnp.where(ux > 0.0, pltpu.roll(f, 1, 1), pltpu.roll(f, nx - 1, 1))
                up_y = jnp.where(uy > 0.0, pltpu.roll(f, 1, 0), pltpu.roll(f, ny - 1, 0))
                up_z = jnp.where(uz > 0.0, below, above)
                moved = f * (1.0 - (ax + ay + az)) + ax * up_x + ay * up_y + az * up_z
                power = (-step_length * terms[0]) * planes[0]
                for c in range(1, 6):
                    power = power + (-step_length * terms[c]) * planes[c]
                res = (moved * jnp.exp(power)).astype(BF16)
                for yb in range(nyb):
                    send1[p, zb * nyb + yb, o] = res[yb * yt : (yb + 1) * yt]

            def ship(j, inner):
                yb = lax.rem(my_yb + 1 + j, nyb)
                d = zb * nyb + yb

                @pl.when(d == me)
                def keep():
                    pltpu.make_async_copy(send1.at[p, d], recv1.at[p, me], sem_r1.at[p]).start()

                @pl.when(d != me)
                def send():
                    left = sem_s1.at[i if p == 0 else nzb]
                    remote(send1.at[p, d], recv1.at[p, me], left, sem_r1.at[p], (sp, d)).start()

                return inner

            if p > 0:
                @pl.when(i < nzb - 1)
                def others_left():
                    sent = send1.at[0, pl.ds(0, nyb)]
                    pltpu.make_async_copy(sent, sent, sem_s1.at[i]).wait()

                @pl.when(i == nzb - 1)
                def own_left():
                    sent = send1.at[0, pl.ds(0, nyb - 1)]
                    pltpu.make_async_copy(sent, sent, sem_s1.at[i]).wait()

            lax.fori_loop(0, nyb, ship, 0)
            turn = p * nzb + i - (zt * nzb - WOVEN)

            @pl.when(turn >= 0)
            def weave():
                ship_part(1 + (EARLY + turn) // zt, lax.rem(EARLY + turn, zt))

            return carry

        lax.fori_loop(0, nzb, advect_plane, 0)

    diagonal = lax.broadcasted_iota(jnp.int32, (no, no), 0) == lax.broadcasted_iota(
        jnp.int32, (no, no), 1
    )
    for a in range(3):
        spread = jnp.where(diagonal, jnp.broadcast_to(dirs_row[pl.ds(a, 1), :], (no, no)), 0.0)
        ub_ref[a] = jnp.broadcast_to(jnp.sum(spread, axis=1, keepdims=True), (no, nx))
    ux = ub_ref[0]
    uy = ub_ref[1]
    uz = ub_ref[2]
    ax = step_length * jnp.abs(ux)
    ay = step_length * jnp.abs(uy)
    az = step_length * jnp.abs(uz)
    cf[0] = 1.0 - (ax + ay + az)
    cf[1] = ax
    cf[2] = ay
    cf[3] = az
    lane = lax.broadcasted_iota(jnp.int32, (no, nx), 1)
    terms = (ux * ux, uy * uy, uz * uz, 2.0 * ux * uy, 2.0 * ux * uz, 2.0 * uy * uz)
    packed = jnp.zeros((no, nx), F32)
    for c in range(6):
        value = -step_length * terms[c]
        high = value.astype(BF16).astype(F32)
        rest = value - high
        middle = rest.astype(BF16).astype(F32)
        low = rest - middle
        packed = jnp.where(lane == c, high, packed)
        packed = jnp.where(lane == 8 + c, middle, packed)
        packed = jnp.where(lane == 16 + c, low, packed)
    ft3[...] = packed.astype(BF16)

    wown[...] = jnp.zeros_like(wown)
    for p in range(zt):
        for c in range(6):
            block = wv[c, my_zb * zt + p, pl.ds(pl.multiple_of(my_yb * yt, yt), yt)]
            wown[pl.ds(p * yt * 8 + c, yt, stride=8), :] = block.astype(F32)

    for p in range(zt):
        pltpu.make_async_copy(recv1.at[p], recv1.at[p], sem_r1.at[p]).wait()

        def widen(s, carry, p=p):
            rows = count * yt
            wide[pl.ds(pl.multiple_of(s * rows, rows), rows), :] = (
                recv1[p, s].astype(F32).reshape(rows, nx)
            )
            return carry

        lax.fori_loop(0, groups, widen, 0, unroll=4)
        for chunk in range(CHUNKS):

            def turn(k, carry, p=p, chunk=chunk):
                y = chunk * per + k
                tile = wide[pl.ds(y, no, stride=yt), :].astype(BF16)
                turned = jnp.dot(rot_ref[...], tile, preferred_element_type=F32)
                ext[p + 1, y + 1] = turned.astype(BF16)
                return carry

            lax.fori_loop(0, per, turn, 0, unroll=2)
            rows = pl.ds(1 + chunk * per, per)
            if p == 0:
                remote(
                    ext.at[1, rows], ext.at[zt + 1, rows], sem_hzs, sem_hz.at[1, chunk], z_prev
                ).start()
            if p == zt - 1:
                remote(
                    ext.at[zt, rows], ext.at[0, rows], sem_hzs, sem_hz.at[0, chunk], z_next
                ).start()
            if chunk == 0:
                remote(
                    ext.at[p + 1, pl.ds(1, 1)],
                    ext.at[p + 1, pl.ds(yt + 1, 1)],
                    sem_hys,
                    sem_hy.at[1, p],
                    y_prev,
                ).start()
            if chunk == CHUNKS - 1:
                remote(
                    ext.at[p + 1, pl.ds(yt, 1)],
                    ext.at[p + 1, pl.ds(0, 1)],
                    sem_hys,
                    sem_hy.at[0, p],
                    y_next,
                ).start()

    ship_parts(EARLY + WOVEN, SOON)

    def factor(i, carry):
        o = (lax.rem(my_zb + i // count, nzb) * nyb + my_yb) * count + lax.rem(i, count)
        gx = dirs[0, o]
        gy = dirs[1, o]
        gz = dirs[2, o]
        gw = weight[o]
        third = 1.0 / 3.0
        tt[0, i] = (gx * gx - third) * gw
        tt[1, i] = (gy * gy - third) * gw
        tt[2, i] = gx * gy * gw
        tt[3, i] = gx * gz * gw
        tt[4, i] = gy * gz * gw
        return carry

    lax.fori_loop(0, nzb * count, factor, 0)

    def await_copy(ref, sem):
        pltpu.make_async_copy(ref, ref, sem).wait()

    def second_step(p, h):
        face = ext.at[p + 1, pl.ds((yt + 1) * h, 1)]
        await_copy(face, sem_hy.at[h, p])
        for chunk in range(h * CHUNKS // 2, (h + 1) * CHUNKS // 2):
            rows = pl.ds(1 + chunk * per, per)
            if p == zt - 1:
                await_copy(ext.at[zt + 1, rows], sem_hz.at[1, chunk])
            if p == 0:
                await_copy(ext.at[0, rows], sem_hz.at[0, chunk])

            def step(k, carry, chunk=chunk):
                y = chunk * per + k
                f = ext[p + 1, y + 1].astype(F32)
                up_x = jnp.where(ub_ref[0] > 0.0, pltpu.roll(f, 1, 1), pltpu.roll(f, nx - 1, 1))
                up_y = jnp.where(
                    ub_ref[1] > 0.0, ext[p + 1, y].astype(F32), ext[p + 1, y + 2].astype(F32)
                )
                up_z = jnp.where(
                    ub_ref[2] > 0.0, ext[p, y + 1].astype(F32), ext[p + 2, y + 1].astype(F32)
                )
                moved = f * cf[0] + cf[1] * up_x + cf[2] * up_y + cf[3] * up_z
                w8 = wown[pl.ds(pl.multiple_of((p * yt + y) * 8, 8), 8), :]
                w24 = jnp.concatenate([w8, w8, w8], axis=0).astype(BF16)
                power = jnp.dot(ft3[:, :24], w24, preferred_element_type=F32)
                adv = (moved * jnp.exp(power)).astype(BF16)
                turned = jnp.dot(rot_ref[...], adv, preferred_element_type=F32)
                wide[pl.ds(y - h * half, no, stride=half), :] = turned
                return carry

            lax.fori_loop(0, per, step, 0)

        for i in Z_ORDER:
            zc = lax.rem(my_yb + i, nyb)

            def pack(r, carry, zc=zc):
                d = lax.rem(my_zb + r, nzb) * nyb + zc
                rows = count * half
                block = wide[pl.ds(pl.multiple_of(d * rows, rows), rows), :]
                send2[p, h, zc, r] = block.astype(BF16).reshape(count, half, nx)
                return carry

            lax.fori_loop(0, nzb, pack, 0, unroll=4)
            src = send2.at[p, h, zc]
            dst = mid.at[p, h, :, :, my_yb]
            if i == 0:
                pltpu.make_async_copy(src, dst, sem_rm.at[p, h]).start()
            else:
                remote(src, dst, sem_sm, sem_rm.at[p, h], (sp, my_zb * nyb + zc)).start()

    def pass_on(p, h):
        await_copy(mid.at[p, h], sem_rm.at[p, h])
        home = out_hbm.at[:, my_zb * zt + p, :, h]
        for r in XY_ORDER:
            src = mid.at[p, h, r]
            if r == 0:
                pltpu.make_async_copy(src, home, sem_ro).start()
            else:
                xy = lax.rem(my_zb + r, nzb)
                remote(src, home, sem_so, sem_ro, (sp, xy * nyb + my_yb)).start()

    def reduce(p, h):
        for g in range(2):
            blocks = pl.ds(g * nyb // 2, nyb // 2)

            def add_terms(r, sums, blocks=blocks):
                for o in range(count):
                    prod = mid[p, h, r, o, blocks].astype(F32)
                    prod = prod * pmid[r, o, p, blocks, h].astype(F32)
                    sums = [sums[c] + tt[c, r * count + o] * prod for c in range(SENT)]
                return tuple(sums)

            zero = jnp.zeros((nyb // 2, half, nx), F32)
            sums = lax.fori_loop(0, nzb, add_terms, (zero,) * SENT, unroll=1)
            for c in range(SENT):
                pt[p, h, blocks, c] = sums[c]
        for i in Z_ORDER:
            zc = lax.rem(my_yb + i, nyb)
            src = pt.at[p, h, zc]
            dst = rs.at[p, h, my_yb]
            if i == 0:
                pltpu.make_async_copy(src, dst, sem_rt.at[p, h]).start()
            else:
                remote(src, dst, sem_st, sem_rt.at[p, h], (sp, my_zb * nyb + zc)).start()

    nf_home = nf_hbm.at[:, pl.ds(my_zb * zt, zt)]
    each = nyb // 2

    def relax(p, h):
        await_copy(rs.at[p, h], sem_rt.at[p, h])
        totals = []
        for c in range(SENT):
            total = rs[p, h, 0, c]
            for s in range(1, nyb):
                total = total + rs[p, h, s, c]
            totals.append(total)
        totals.insert(2, -(totals[0] + totals[1]))
        for c in range(6):
            total = totals[c]
            old = wv[c, my_zb * zt + p, pl.ds(pl.multiple_of(my_yb * yt, yt), yt)].astype(F32)
            old = old[h * half : (h + 1) * half]
            value = (1.0 - relax_rate) * old + relax_rate * coupling * total
            for j in range(each):
                nfb[h * each + j, c, p] = value[2 * j : 2 * j + 2]
        if p == 0:

            def ship_field(j, carry):
                k = my_yb * nyb + j

                @pl.when(k == me)
                def keep():
                    pltpu.make_async_copy(nfb.at[j], nf_home, sem_rn).start()

                @pl.when(k != me)
                def send():
                    remote(nfb.at[j], nf_home, sem_sn, sem_rn, (sp, k)).start()

                return carry

            lax.fori_loop(h * each, (h + 1) * each, ship_field, 0)

    second_step(1, 0)
    second_step(1, 1)
    ship_parts(SOON, (nzb - 1) * zt)
    second_step(0, 0)
    second_step(0, 1)
    pass_on(1, 0)
    await_copy(pmid, sem_rp)
    reduce(1, 0)
    pass_on(1, 1)
    reduce(1, 1)
    pass_on(0, 0)
    reduce(0, 0)
    pass_on(0, 1)
    reduce(0, 1)
    relax(1, 0)
    relax(1, 1)
    relax(0, 0)
    relax(0, 1)

    def drain(ref, sem):
        pltpu.make_async_copy(ref, ref, sem).wait()

    drain(nf_hbm, sem_rn)
    drain(out_hbm, sem_ro)
    drain(qext.at[:, pl.ds(0, 2)], sem_hqs)
    drain(send1.at[1, pl.ds(0, groups - 1)], sem_s1.at[nzb])
    drain(pmid.at[pl.ds(0, nzb - 1)], sem_sp)
    drain(ext.at[pl.ds(0, 2), pl.ds(1, yt)], sem_hzs)
    drain(ext.at[0, pl.ds(0, 4)], sem_hys)
    drain(send2.at[:, :, pl.ds(0, nyb - 1)], sem_sm)
    drain(mid.at[:, :, pl.ds(0, nzb - 1)], sem_so)
    drain(pt.at[:, :, pl.ds(0, nyb - 1)], sem_st)

    sent_self = my_zb == my_yb

    @pl.when(sent_self)
    def drain_most():
        drain(nfb.at[pl.ds(0, nyb - 1)], sem_sn)

    @pl.when(jnp.logical_not(sent_self))
    def drain_all():
        drain(nfb, sem_sn)


def per_device(q_init, partner, field, orientations, orient_weight, rotation):
    count, nz, ny, nx = q_init.shape
    no = orientations.shape[1]
    nzb, nyb = nz // ZT, ny // YT
    groups = lax.axis_size("orient")
    spaces = lax.axis_size("space")
    dims = (spaces, groups, nzb, nyb, count, nz, ny, nx)
    pairs = ny // groups
    hbm = pl.BlockSpec(memory_space=pltpu.HBM)
    anywhere = pl.BlockSpec(memory_space=pltpu.VMEM)
    dma = pltpu.SemaphoreType.DMA
    part = partner.reshape(count, nz, nyb, 2, YT // 2, nx)
    out, new_field = pl.pallas_call(
        functools.partial(whole_kernel, dims),
        in_specs=[hbm] * 6,
        out_specs=[anywhere, anywhere],
        out_shape=[
            jax.ShapeDtypeStruct((count, nz, nyb, 2, YT // 2, nx), BF16),
            jax.ShapeDtypeStruct((6, nz, pairs, nx), F32),
        ],
        scratch_shapes=[
            pltpu.VMEM((no, no), BF16),
            pltpu.VMEM((3, no), F32),
            pltpu.SMEM((3, no), F32),
            pltpu.SMEM((no,), F32),
            pltpu.VMEM((3, no, nx), F32),
            pltpu.VMEM((count, nz + 2, ny, nx), BF16),
            pltpu.VMEM((6, nz, ny, nx), BF16),
            pltpu.VMEM((ZT, groups, count, YT, nx), BF16),
            pltpu.VMEM((ZT, groups, count, YT, nx), BF16),
            pltpu.VMEM((ZT + 2, YT + 2, no, nx), BF16),
            pltpu.VMEM((no * YT, nx), F32),
            pltpu.VMEM((nzb, count, ZT, nyb, 2, YT // 2, nx), BF16),
            pltpu.VMEM((ZT, 2, nyb, nzb, count, YT // 2, nx), BF16),
            pltpu.VMEM((ZT, 2, nzb, count, nyb, YT // 2, nx), BF16),
            pltpu.VMEM((ZT, 2, nyb, SENT, YT // 2, nx), F32),
            pltpu.VMEM((ZT, 2, nyb, SENT, YT // 2, nx), F32),
            pltpu.SMEM((SENT, nzb * count), F32),
            pltpu.VMEM((nyb, 6, ZT, pairs, nx), F32),
            pltpu.VMEM((4, no, nx), F32),
            pltpu.VMEM((no, nx), BF16),
            pltpu.VMEM((ZT * YT * 8, nx), F32),
            dma((6,)),
            dma((2,)),
            dma(()),
            dma((ZT,)),
            dma((nzb + 1,)),
            dma(()),
            dma(()),
            dma((2, CHUNKS)),
            dma(()),
            dma((2, ZT)),
            dma(()),
            dma((ZT, 2)),
            dma(()),
            dma(()),
            dma(()),
            dma((ZT, 2)),
            dma(()),
            dma(()),
            dma(()),
        ],
        compiler_params=pltpu.CompilerParams(
            collective_id=0, has_side_effects=True, vmem_limit_bytes=40 << 20
        ),
        name="whole",
    )(
        *[
            pltpu.with_memory_space_constraint(x, pltpu.HBM)
            for x in (q_init, part, field, rotation, orientations, orient_weight)
        ]
    )
    return out.reshape(count, nz, ny, nx), new_field


def solution(mesh):
    in_specs = (
        P("orient", "space", None, None),
        P("orient", "space", None, None),
        P(None, "space", None, None),
        P(),
        P(),
        P(),
    )
    out_specs = (P("orient", "space", None, None), P(None, "space", "orient", None))
    return jax.shard_map(
        per_device, mesh=mesh, in_specs=in_specs, out_specs=out_specs, check_vma=False
    )
```
